128 devices in a mesh: gx: 16 (over z, x), gy: 8 (over y, core).
Axes of the slice: x: 4, y: 4, z: 4, core: 2. Of those that a mesh axis runs over, the one named last changes fastest.
Arguments:
- inputs: float32 [128, 64, 16, 256], P('gx', 'gy'), may hold values from -6 to 6
- cotangent: float32 [128, 64, 16, 256], P('gx', 'gy'), may hold values from -6 to 6
- weight: float32 [6912, 256], replicated, may hold values from -0.125 to 0.125
- occupancy: int32 [128, 64, 16], P('gx', 'gy'), may hold values from 0 to 1, as said below
Outputs:
- input_grad: float32 [128, 64, 16, 256], P('gx', 'gy')
- weight_grad: float32 [6912, 256], P('gx', 'gy')
The draws below stay inside these ranges and needn't reach their ends.
Inputs may be any that keep to these rules, and one draw needn't show every extreme that they name: `occupancy`: occupied voxels lie in bricks of 8 x 8 x min(8, 16) voxels aligned to each device's block; some bricks are empty.
All inputs are finite; a program needn't handle non-finite values.
Results may differ from the reference program's by a relative error of at most 0.0001.
Values sent between devices are 32-bit elements; how exact they have to be, the bound alone decides.
A program may use at most 192 MiB of HBM per device.

```python
import jax
import jax.numpy as jnp
from jax import lax

C = 256
CX = 8
CY = 8
NX = 128
NY = 64
NZ = 16


def draw_occupancy(key, part):
    brick_depth = min(8, NZ)
    count_x = NX // CX
    count_y = NY // CY
    count_z = NZ // brick_depth
    level_key = jax.random.fold_in(key, 11)
    brick_key = jax.random.fold_in(key, 12)
    dense_key = jax.random.fold_in(key, 13)
    voxel_key = jax.random.fold_in(key, 14)
    device_level = jax.random.randint(level_key, (count_x, count_y, 1), 3, 7)
    brick_score = jax.random.randint(brick_key, (count_x, count_y, count_z), 0, 10)
    brick_live = (brick_score < device_level).astype(jnp.int32)
    brick_dense = jax.random.randint(dense_key, (count_x, count_y, count_z), 1, 4) * brick_live
    dense_full = jnp.repeat(jnp.repeat(jnp.repeat(brick_dense, CX, axis=0), CY, axis=1), brick_depth, axis=2)
    voxel_score = jax.random.randint(voxel_key, (NX, NY, NZ), 0, 10)
    result = (voxel_score < dense_full).astype(jnp.int32)
    result = result.at[0, 0, 0].set(1)
    result = result.at[0, 0, 1].set(0)
    return result


def block_levels(own_key, shape, cuts, low, high):
    def one(position, shards_of):
        steps = jax.random.uniform(jax.random.fold_in(jax.random.fold_in(own_key, 6), position), (shards_of,), jnp.float32, low / len(cuts), high / len(cuts))
        return jnp.repeat(jnp.exp(steps), shape[position] // shards_of).reshape((-1,) + (1,) * (len(shape) - position - 1))

    level = one(*cuts[0])
    for cut in cuts[1:]:
        level = level * one(*cut)
    return level


def normal_values(rng, shape, deviation, most, pieces=(), dtype=jnp.bfloat16):
    gain = block_levels(rng, shape, pieces, -0.22, 0.18) if pieces else 1.0
    array = jax.random.normal(rng, shape, jnp.float32) * deviation * gain
    return jnp.minimum(jnp.maximum(array, -most), most).astype(dtype)


def setup_inputs(seed: int = 0) -> dict:
    key_of = jax.random.split(jax.random.key(seed), 5)
    return {
        "inputs": normal_values(key_of[0], (NX, NY, NZ, C), 1.0, 6.0, ((0, 16), (1, 8)), jnp.float32),
        "cotangent": normal_values(key_of[1], (NX, NY, NZ, C), 1.0, 6.0, ((0, 16), (1, 8)), jnp.float32),
        "weight": normal_values(key_of[2], (27 * C, C), (9 * C) ** -0.5, 0.125, (), jnp.float32),
        "occupancy": draw_occupancy(jax.random.fold_in(key_of[4], 71), 0),
    }


def offsets():
    return [(first, second, third) for first in range(3) for second in range(3) for third in range(3)]


def reference(inputs, cotangent, weight, occupancy):
    filled = occupancy.astype(jnp.float32)[..., None]
    masked = inputs * filled
    padded = jnp.pad(masked, ((1, 1), (1, 1), (1, 1), (0, 0)))
    total_rows = NX * NY * NZ
    preact = jnp.zeros((total_rows, C), jnp.float32)
    for index, (first, second, third) in enumerate(offsets()):
        piece = padded[first:first + NX, second:second + NY, third:third + NZ].reshape(total_rows, C)
        preact = preact + jnp.dot(piece, weight[index * C:(index + 1) * C], precision=lax.Precision.HIGHEST, preferred_element_type=jnp.float32)
    sigma = jax.nn.sigmoid(preact)
    upstream = cotangent.reshape(total_rows, C) * sigma * (1.0 + preact * (1.0 - sigma)) * filled.reshape(total_rows, 1)
    grid_up = jnp.pad(upstream.reshape(NX, NY, NZ, C), ((1, 1), (1, 1), (1, 1), (0, 0)))
    result = jnp.zeros((total_rows, C), jnp.float32)
    blocks = []
    for index, (first, second, third) in enumerate(offsets()):
        kernel = weight[index * C:(index + 1) * C]
        back = grid_up[2 - first:2 - first + NX, 2 - second:2 - second + NY, 2 - third:2 - third + NZ].reshape(total_rows, C)
        result = result + jnp.dot(back, kernel.T, precision=lax.Precision.HIGHEST, preferred_element_type=jnp.float32)
        piece = padded[first:first + NX, second:second + NY, third:third + NZ].reshape(total_rows, C)
        blocks.append(jnp.dot(piece.T, upstream, precision=lax.Precision.HIGHEST, preferred_element_type=jnp.float32))
    input_grad = (result * filled.reshape(total_rows, 1)).reshape(NX, NY, NZ, C)
    return input_grad, jnp.concatenate(blocks, axis=0)
```

```python
import jax, jax.numpy as jnp
from jax import lax
from jax.experimental import pallas as pl
from jax.experimental.pallas import tpu as pltpu
from jax.sharding import Mesh
from jax.sharding import PartitionSpec as P

GX = ("gx_0", "gx_1")
F32 = jnp.float32
BF16 = jnp.bfloat16


def split(value):
    high = value.astype(BF16)
    return high, (value - high.astype(F32)).astype(BF16)


def rows(index, size):
    return pl.ds(pl.multiple_of(index * size, size), size)


def filter_points(a, b, c):
    outer, inner = (a + c) * 0.5, b * 0.5
    return a, outer + inner, outer - inner, c


def data_points(a, b, c, d):
    return a - c, b + c, c - b, b - d


def sums_of_points(a, b, c, d):
    return a + b + c, b - c - d


def points_of_pair(a, b):
    return a, a + b, a - b, -b


def taps_of_points(a, b, c, d):
    outer = (b + c) * 0.5
    return a + outer, (b - c) * 0.5, outer + d


def both(function, grid):
    half = list(zip(*[function(*column) for column in zip(*grid)]))
    return [function(*row) for row in half]


def transform_weight(weight, high, low):
    def step(index, carry):
        grid = [
            [weight[pl.ds(pl.multiple_of((3 * a + b) * 768 + index * 16, 16), 16)] for b in range(3)]
            for a in range(3)
        ]
        points = both(filter_points, grid)
        for u in range(4):
            for v in range(4):
                top, rest = split(points[u][v])
                high[4 * u + v, rows(index, 16)] = top
                low[4 * u + v, rows(index, 16)] = rest
        return carry

    lax.fori_loop(0, 48, step, 0)


def transform_data(padded, high, low):
    def step(tile, carry):
        x, y = tile // 4, tile % 4
        grid = [[padded[2 * x + i, 2 * y + j] for j in range(4)] for i in range(4)]
        points = both(data_points, grid)
        zero = jnp.zeros((1, 256), F32)
        for u in range(4):
            for v in range(4):
                mid = points[u][v]
                down = jnp.concatenate([zero, mid[:15]], axis=0)
                up = jnp.concatenate([mid[1:], zero], axis=0)
                for place, piece in enumerate((down, mid, up)):
                    top, rest = split(piece)
                    high[4 * u + v, rows(tile, 16), 256 * place : 256 * place + 256] = top
                    low[4 * u + v, rows(tile, 16), 256 * place : 256 * place + 256] = rest
        return carry

    lax.fori_loop(0, 16, step, 0)


def dots(left_high, left_low, right_high, right_low, numbers):
    dims = (numbers, ((), ()))
    return (
        lax.dot_general(left_high, right_high, dims, preferred_element_type=F32)
        + lax.dot_general(left_low, right_high, dims, preferred_element_type=F32)
        + lax.dot_general(left_high, right_low, dims, preferred_element_type=F32)
    )


def forward(data_high, data_low, filter_high, filter_low, product):
    def step(point, carry):
        product[point] = dots(
            data_high[point], data_low[point], filter_high[point], filter_low[point], ((1,), (0,))
        )
        return carry

    lax.fori_loop(0, 16, step, 0)


def backward(data_high, data_low, filter_high, filter_low, product):
    def step(point, carry):
        u, v = point // 4, point % 4
        u = jnp.where(u == 0, 3, jnp.where(u == 3, 0, u))
        v = jnp.where(v == 0, 3, jnp.where(v == 3, 0, v))
        other = 4 * u + v
        total = None
        for place in range(3):
            lanes = slice(256 * place, 256 * place + 256)
            taps = slice(256 * (2 - place), 256 * (2 - place) + 256)
            term = dots(
                data_high[point, :, lanes],
                data_low[point, :, lanes],
                filter_high[other, taps],
                filter_low[other, taps],
                ((1,), (1,)),
            )
            total = term if total is None else total + term
        product[point] = total
        return carry

    lax.fori_loop(0, 16, step, 0)


def upstream_of(product, cotangent, filled, grid_up, up_high, up_low):
    def step(tile, carry):
        x, y = tile // 4, tile % 4
        grid = [[product[4 * u + v, rows(tile, 16)] for v in range(4)] for u in range(4)]
        sums = both(sums_of_points, grid)
        pair = []
        for i in range(2):
            line = []
            for j in range(2):
                value = sums[i][j]
                sigma = 1.0 / (1.0 + jnp.exp(-value))
                fill = filled[2 * x + i, 2 * y + j]
                fill = jnp.concatenate([fill, fill], axis=1)
                result = cotangent[2 * x + i, 2 * y + j] * sigma * (1.0 + value * (1.0 - sigma)) * fill
                grid_up[2 * x + i, 2 * y + j] = result
                line.append(result)
            pair.append(line)
        points = both(points_of_pair, pair)
        for u in range(4):
            for v in range(4):
                top, rest = split(points[u][v])
                up_high[4 * u + v, rows(tile, 16)] = top
                up_low[4 * u + v, rows(tile, 16)] = rest
        return carry

    lax.fori_loop(0, 16, step, 0)


def weight_terms(data_high, data_low, up_high, up_low, product, term):
    for place in range(3):
        lanes = slice(256 * place, 256 * place + 256)

        def step(point, carry):
            product[point] = dots(
                data_high[point, :, lanes], data_low[point, :, lanes], up_high[point], up_low[point], ((0,), (0,))
            )
            return carry

        lax.fori_loop(0, 16, step, 0)

        def gather(index, carry):
            grid = [[product[4 * u + v, rows(index, 16)] for v in range(4)] for u in range(4)]
            taps = both(taps_of_points, grid)
            for a in range(3):
                for b in range(3):
                    start = (3 * a + b) * 768 + 256 * place
                    term[pl.ds(pl.multiple_of(start + index * 16, 16), 16)] = taps[a][b]
            return carry

        lax.fori_loop(0, 16, gather, 0)


def result_of(product, filled, result):
    def step(tile, carry):
        x, y = tile // 4, tile % 4
        grid = [[product[4 * u + v, rows(tile, 16)] for v in range(4)] for u in range(4)]
        sums = both(sums_of_points, grid)
        for i in range(2):
            for j in range(2):
                fill = filled[2 * x + i, 2 * y + j]
                result[2 * x + i, 2 * y + j] = sums[i][j] * jnp.concatenate([fill, fill], axis=1)
        return carry

    lax.fori_loop(0, 16, step, 0)


def first_kernel(padded, cotangent, filled, weight, grid_up, term, dh, dl, fh, fl, eh, el, product):
    transform_weight(weight, fh, fl)
    transform_data(padded, dh, dl)
    forward(dh, dl, fh, fl, product)
    upstream_of(product, cotangent, filled, grid_up, eh, el)
    weight_terms(dh, dl, eh, el, product, term)


def second_kernel(padded, filled, weight, result, dh, dl, fh, fl, product):
    transform_weight(weight, fh, fl)
    transform_data(padded, dh, dl)
    backward(dh, dl, fh, fl, product)
    result_of(product, filled, result)


IN_VMEM = pl.BlockSpec(memory_space=pltpu.VMEM)
PARAMS = pltpu.CompilerParams(vmem_limit_bytes=63 << 20)
DATA = [pltpu.VMEM((16, 256, 768), BF16)] * 2
FILTER = [pltpu.VMEM((16, 768, 256), BF16)] * 2
PRODUCT = [pltpu.VMEM((16, 256, 256), F32)]


def run_first(padded, cotangent, filled, weight):
    return pl.pallas_call(
        first_kernel,
        out_shape=(jax.ShapeDtypeStruct((8, 8, 16, 256), F32), jax.ShapeDtypeStruct((6912, 256), F32)),
        in_specs=[IN_VMEM] * 4,
        out_specs=(IN_VMEM, IN_VMEM),
        scratch_shapes=DATA + FILTER + [pltpu.VMEM((16, 256, 256), BF16)] * 2 + PRODUCT,
        compiler_params=PARAMS,
        name="first",
    )(padded, cotangent, filled, weight)


def run_second(padded, filled, weight):
    return pl.pallas_call(
        second_kernel,
        out_shape=jax.ShapeDtypeStruct((8, 8, 16, 256), F32),
        in_specs=[IN_VMEM] * 3,
        out_specs=IN_VMEM,
        scratch_shapes=DATA + FILTER + PRODUCT,
        compiler_params=PARAMS,
        name="second",
    )(padded, filled, weight)


def with_halo(array, sides, width):
    for axis, dim in sides:
        devices, length = (lax.axis_size(axis), array.shape[dim])
        up = [(i, (i + 1) % devices) for i in range(devices - 1)]
        down = [(j, i) for i, j in up]
        last = lax.slice_in_dim(array, length - width, length, axis=dim)
        first = lax.slice_in_dim(array, 0, width, axis=dim)
        before = lax.ppermute(last, axis, up)
        after = lax.ppermute(first, axis, down)
        array = jnp.concatenate([before, array, after], axis=dim)
    return array


def sum_by_axis(array, axes, dim):
    for axis in axes:
        array = lax.psum_scatter(array, axis, scatter_dimension=dim, tiled=True)
    return array


def cut_along(array, dim, devices):
    shape = array.shape
    tiles = array.reshape(*shape[:dim], devices, shape[dim] // devices, *shape[dim + 1 :])
    return jnp.moveaxis(tiles, dim, 0)


def sent_and_summed(array, axis, dim):
    devices = lax.axis_size(axis)
    tiles = lax.all_to_all(cut_along(array, dim, devices), axis, 0, 0, tiled=True)
    return jnp.sum(tiles, axis=0)


def body(inputs, cotangent, weight, occupancy):
    filled = occupancy.astype(F32)[..., None]
    masked = inputs * filled
    wide = jnp.broadcast_to(filled, (*occupancy.shape, 128))
    bordered = with_halo(masked, ((GX, 0), ("gy", 1)), 1)
    grid_up, term = run_first(bordered, cotangent, wide, weight)
    row_sums = sum_by_axis(term, GX, 0)
    border_up = with_halo(grid_up, ((GX, 0), ("gy", 1)), 1)
    input_grad = run_second(border_up, wide, weight)
    weight_grad = sent_and_summed(row_sums, "gy", 1)
    return (input_grad, weight_grad)


def solution(mesh):
    split_mesh = Mesh(mesh.devices.reshape(4, 4, mesh.shape["gy"]), ("gx_0", "gx_1", "gy"))
    in_specs = (P(GX, "gy", None, None), P(GX, "gy", None, None), P(), P(GX, "gy", None))
    out_specs = (P(GX, "gy", None, None), P(GX, "gy"))
    return jax.shard_map(body, mesh=split_mesh, in_specs=in_specs, out_specs=out_specs, check_vma=False)
```

```python
import jax, jax.numpy as jnp
from jax import lax
from jax.experimental import pallas as pl
from jax.experimental.pallas import tpu as pltpu
from jax.sharding import PartitionSpec as P

F32 = jnp.float32
BF16 = jnp.bfloat16


def split(value):
    high = value.astype(BF16)
    return high, (value - high.astype(F32)).astype(BF16)


def rows(index, size):
    return pl.ds(pl.multiple_of(index * size, size), size)


def filter_points(a, b, c):
    outer, inner = (a + c) * 0.5, b * 0.5
    return a, outer + inner, outer - inner, c


def data_points(a, b, c, d):
    return a - c, b + c, c - b, b - d


def sums_of_points(a, b, c, d):
    return a + b + c, b - c - d


def points_of_pair(a, b):
    return a, a + b, a - b, -b


def taps_of_points(a, b, c, d):
    outer = (b + c) * 0.5
    return a + outer, (b - c) * 0.5, outer + d


def both(function, grid):
    half = list(zip(*[function(*column) for column in zip(*grid)]))
    return [function(*row) for row in half]


def transform_weight(weight, high, low):
    def step(index, carry):
        grid = [
            [weight[pl.ds(pl.multiple_of((3 * a + b) * 768 + index * 16, 16), 16)] for b in range(3)]
            for a in range(3)
        ]
        points = both(filter_points, grid)
        for u in range(4):
            for v in range(4):
                top, rest = split(points[u][v])
                high[4 * u + v, rows(index, 16)] = top
                low[4 * u + v, rows(index, 16)] = rest
        return carry

    lax.fori_loop(0, 48, step, 0)


def transform_data(padded, high, low):
    def step(tile, carry):
        x, y = tile // 4, tile % 4
        grid = [[padded[2 * x + i, 2 * y + j] for j in range(4)] for i in range(4)]
        points = both(data_points, grid)
        zero = jnp.zeros((1, 256), F32)
        for u in range(4):
            for v in range(4):
                mid = points[u][v]
                down = jnp.concatenate([zero, mid[:15]], axis=0)
                up = jnp.concatenate([mid[1:], zero], axis=0)
                for place, piece in enumerate((down, mid, up)):
                    top, rest = split(piece)
                    high[4 * u + v, rows(tile, 16), 256 * place : 256 * place + 256] = top
                    low[4 * u + v, rows(tile, 16), 256 * place : 256 * place + 256] = rest
        return carry

    lax.fori_loop(0, 16, step, 0)


def dots(left_high, left_low, right_high, right_low, numbers):
    dims = (numbers, ((), ()))
    return (
        lax.dot_general(left_high, right_high, dims, preferred_element_type=F32)
        + lax.dot_general(left_low, right_high, dims, preferred_element_type=F32)
        + lax.dot_general(left_high, right_low, dims, preferred_element_type=F32)
    )


def forward(data_high, data_low, filter_high, filter_low, product):
    def step(point, carry):
        product[point] = dots(
            data_high[point], data_low[point], filter_high[point], filter_low[point], ((1,), (0,))
        )
        return carry

    lax.fori_loop(0, 16, step, 0)


def backward(data_high, data_low, filter_high, filter_low, product):
    def step(point, carry):
        u, v = point // 4, point % 4
        u = jnp.where(u == 0, 3, jnp.where(u == 3, 0, u))
        v = jnp.where(v == 0, 3, jnp.where(v == 3, 0, v))
        other = 4 * u + v
        total = None
        for place in range(3):
            lanes = slice(256 * place, 256 * place + 256)
            taps = slice(256 * (2 - place), 256 * (2 - place) + 256)
            term = dots(
                data_high[point, :, lanes],
                data_low[point, :, lanes],
                filter_high[other, taps],
                filter_low[other, taps],
                ((1,), (1,)),
            )
            total = term if total is None else total + term
        product[point] = total
        return carry

    lax.fori_loop(0, 16, step, 0)


def place_lanes(value):
    left, right = value[:, :128], value[:, 128:]
    group = lax.broadcasted_iota(jnp.int32, left.shape, 1) // 32
    left_32, right_32 = pltpu.roll(left, 96, 1), pltpu.roll(right, 32, 1)
    left_64, right_64 = pltpu.roll(left, 64, 1), pltpu.roll(right, 64, 1)
    even = jnp.where(group == 0, left, jnp.where(group == 1, left_32, jnp.where(group == 2, right_64, right_32)))
    odd = jnp.where(group == 0, left_32, jnp.where(group == 1, left_64, jnp.where(group == 2, right_32, right)))
    return jnp.concatenate([even, odd], axis=1)


def transform_filter(weight, high, low):
    def step(index, carry):
        def piece(tap):
            start = tap * 96 + index * 2
            return jnp.concatenate(
                [weight[half, pl.ds(start, 2)].reshape(16, 128) for half in range(2)], axis=1
            )

        points = both(filter_points, [[piece(3 * a + b) for b in range(3)] for a in range(3)])
        for u in range(4):
            for v in range(4):
                top, rest = split(points[u][v])
                high[4 * u + v, rows(index, 16)] = top
                low[4 * u + v, rows(index, 16)] = rest
        return carry

    lax.fori_loop(0, 48, step, 0)


def backward_points(data_high, data_low, filter_high, filter_low, product, first, last):
    def step(point, carry):
        u, v = point // 4, point % 4
        u = jnp.where(u == 0, 3, jnp.where(u == 3, 0, u))
        v = jnp.where(v == 0, 3, jnp.where(v == 3, 0, v))
        other = 4 * u + v
        total = None
        for place in range(3):
            lanes = slice(256 * place, 256 * place + 256)
            taps = slice(256 * (2 - place), 256 * (2 - place) + 256)
            term = dots(
                data_high[point, :, lanes],
                data_low[point, :, lanes],
                filter_high[other, taps],
                filter_low[other, taps],
                ((1,), (1,)),
            )
            total = term if total is None else total + term
        product[point] = total
        return carry

    lax.fori_loop(first, last, step, 0)


def twice(fill):
    return jnp.concatenate([fill, fill], axis=1)


def upstream_of(product, cotangent, filled, grid_up, up_high, up_low):
    def step(tile, carry):
        x, y = tile // 4, tile % 4
        grid = [[product[4 * u + v, rows(tile, 16)] for v in range(4)] for u in range(4)]
        sums = both(sums_of_points, grid)
        pair = []
        for i in range(2):
            line = []
            for j in range(2):
                value = sums[i][j]
                sigma = 1.0 / (1.0 + jnp.exp(-value))
                fill = twice(filled[2 * x + i, 2 * y + j])
                result = cotangent[2 * x + i, 2 * y + j] * sigma * (1.0 + value * (1.0 - sigma)) * fill
                grid_up[2 * x + i + 1, 2 * y + j + 1] = result
                line.append(place_lanes(result))
            pair.append(line)
        points = both(points_of_pair, pair)
        for u in range(4):
            for v in range(4):
                top, rest = split(points[u][v])
                up_high[4 * u + v, rows(tile, 16)] = top
                up_low[4 * u + v, rows(tile, 16)] = rest
        return carry

    lax.fori_loop(0, 16, step, 0)


def weight_points(data_high, data_low, up_high, up_low, product, place, first, count):
    lanes = slice(256 * place, 256 * place + 256)

    def step(index, carry):
        point = first + index
        product[index] = dots(
            data_high[point, :, lanes], data_low[point, :, lanes], up_high[point], up_low[point], ((0,), (0,))
        )
        return carry

    lax.fori_loop(0, count, step, 0)


def store_taps(term, a, place, index, taps, add):
    for b in range(3):
        start = ((3 * a + b) * 3 + place) * 32 + 2 * index
        for half in range(2):
            value = taps[b][:, 128 * half : 128 * half + 128].reshape(2, 8, 128)
            if add:
                value = value + term[half, pl.ds(start, 2)]
            term[half, pl.ds(start, 2)] = value


def middle_taps(product, term, place):
    def step(index, carry):
        one = [product[v, rows(index, 16)] for v in range(4)]
        two = [product[4 + v, rows(index, 16)] for v in range(4)]
        outer = taps_of_points(*[(p + q) * 0.5 for p, q in zip(one, two)])
        inner = taps_of_points(*[(p - q) * 0.5 for p, q in zip(one, two)])
        store_taps(term, 0, place, index, outer, False)
        store_taps(term, 1, place, index, inner, False)
        store_taps(term, 2, place, index, outer, False)
        return carry

    lax.fori_loop(0, 16, step, 0)


def outer_taps(product, term, place, a):
    def step(index, carry):
        taps = taps_of_points(*[product[v, rows(index, 16)] for v in range(4)])
        store_taps(term, a, place, index, taps, True)
        return carry

    lax.fori_loop(0, 16, step, 0)


def result_of(product, filled, result):
    def step(tile, carry):
        x, y = tile // 4, tile % 4
        grid = [[product[4 * u + v, rows(tile, 16)] for v in range(4)] for u in range(4)]
        sums = both(sums_of_points, grid)
        for i in range(2):
            for j in range(2):
                result[2 * x + i, 2 * y + j] = sums[i][j] * twice(filled[2 * x + i, 2 * y + j])
        return carry

    lax.fori_loop(0, 16, step, 0)


def fill_of(occupancy, filled):
    same = lax.broadcasted_iota(jnp.int32, (16, 16), 0) == lax.broadcasted_iota(jnp.int32, (16, 16), 1)

    def step(x, carry):
        level = occupancy[x].astype(F32)
        for y in range(8):
            line = jnp.where(same, jnp.broadcast_to(level[y : y + 1], (16, 16)), 0.0)
            filled[x, y] = jnp.broadcast_to(jnp.sum(line, axis=1, keepdims=True), (16, 128))
        return carry

    lax.fori_loop(0, 8, step, 0)


def mask_data(padded, filled):
    def step(index, carry):
        x, y = index // 8, index % 8
        padded[x + 1, y + 1] = padded[x + 1, y + 1] * twice(filled[x, y])
        return carry

    lax.fori_loop(0, 64, step, 0)


MESH = pl.DeviceIdType.MESH
AROUND = [(i, j) for i in (-1, 0, 1) for j in (-1, 0, 1) if (i, j) != (0, 0)]


def strip(step):
    source = {-1: 1, 0: pl.ds(1, 8), 1: 8}[step]
    target = {-1: 9, 0: pl.ds(1, 8), 1: 0}[step]
    return source, target


def border_copies(grid, send, recv, gx, gy):
    copies = []
    for index, (i, j) in enumerate(AROUND):
        (from_x, to_x), (from_y, to_y) = strip(i), strip(j)
        copies.append(
            pltpu.make_async_remote_copy(
                grid.at[from_x, from_y],
                grid.at[to_x, to_y],
                send.at[index],
                recv.at[index],
                device_id=((gx + i + 16) % 16, (gy + j + 8) % 8),
                device_id_type=MESH,
            )
        )
    return copies


def clear_edges(grid, gx, gy):
    @pl.when(gx == 0)
    def _():
        grid[0] = jnp.zeros((10, 16, 256), F32)

    @pl.when(gx == 15)
    def _():
        grid[9] = jnp.zeros((10, 16, 256), F32)

    @pl.when(gy == 0)
    def _():
        for x in range(10):
            grid[x, 0] = jnp.zeros((16, 256), F32)

    @pl.when(gy == 7)
    def _():
        for x in range(10):
            grid[x, 9] = jnp.zeros((16, 256), F32)


def kernel(
    inputs, cotangent, weight, occupancy, result, weight_grad,
    term, fh, fl, dh, dl, eh, el, product, padded, padded_up, cot, filled, occ,
    from_core, ring_slots, cross_first, cross_next, packed, packed_in, out, final,
    local, border_send, border_recv, up_send, up_recv, core_send, core_recv,
    ring_send, ring_recv, cross_send, cross_recv, column_send, column_recv,
):
    gx, gy = lax.axis_index("gx"), lax.axis_index("gy")
    z, x, y, c = gx // 4, gx % 4, gy // 2, gy % 2

    load_inputs = pltpu.make_async_copy(inputs, padded.at[pl.ds(1, 8), pl.ds(1, 8)], local.at[0])
    load_occ = pltpu.make_async_copy(occupancy, occ, local.at[1])
    load_weight = [
        pltpu.make_async_copy(weight.at[:, :, pl.ds(128 * half, 128)], term.at[half], local.at[2 + half])
        for half in range(2)
    ]
    load_cot = pltpu.make_async_copy(cotangent, cot, local.at[4])
    for copy in (load_occ, load_inputs, *load_weight, load_cot):
        copy.start()

    def at(new_z, new_x, new_y):
        return (4 * ((new_z + 4) % 4) + (new_x + 4) % 4, 2 * ((new_y + 4) % 4) + c)

    partners = [((gx + i + 16) % 16, (gy + j + 8) % 8) for i, j in AROUND]
    partners += [(gx, 2 * y + 1 - c)]
    partners += [at(z + 1, x, y), at(z - 1, x, y), at(z, x + 1, y), at(z, x - 1, y)]
    partners += [at(z, x, y + 1), at(z, x, y + 2), at(z, x, y + 3)]
    barrier = pltpu.get_barrier_semaphore()
    for partner in partners:
        pl.semaphore_signal(barrier, inc=1, device_id=partner, device_id_type=MESH)

    load_occ.wait()
    fill_of(occ, filled)
    load_inputs.wait()
    mask_data(padded, filled)
    pl.semaphore_wait(barrier, len(partners))
    borders = border_copies(padded, border_send, border_recv, gx, gy)
    for copy in borders:
        copy.start()
    for copy in load_weight:
        copy.wait()
    transform_filter(term, fh, fl)
    for copy in borders:
        copy.wait()
    clear_edges(padded, gx, gy)
    transform_data(padded, dh, dl)
    forward(dh, dl, fh, fl, product)
    load_cot.wait()
    upstream_of(product, cot, filled, padded_up, eh, el)
    borders = border_copies(padded_up, up_send, up_recv, gx, gy)
    for copy in borders:
        copy.start()

    def to_core(a):
        taps = pl.ds(288 * a, 288)
        return pltpu.make_async_remote_copy(
            term.at[1 - c, taps], from_core.at[taps], core_send.at[a], core_recv.at[a],
            device_id=(gx, 2 * y + 1 - c), device_id_type=MESH,
        )

    def add_core(a):
        def step(index, carry):
            tiles = pl.ds(288 * a + 16 * index, 16)
            term[c, tiles] = term[c, tiles] + from_core[tiles]
            return carry

        lax.fori_loop(0, 18, step, 0)

    core_copies = {}
    for a, first, count in ((1, 4, 8), (0, 0, 4), (2, 12, 4)):
        for place in range(3):
            weight_points(dh, dl, eh, el, product, place, first, count)
            if a == 1:
                middle_taps(product, term, place)
            else:
                outer_taps(product, term, place, a)
        core_copies[a] = to_core(a)
        core_copies[a].start()
    for a in (1, 0, 2):
        core_copies[a].wait_recv()
        add_core(a)

    def tiles_of(path, ring, cross, start=0, size=27):
        block = 4 * ((ring + 4) % 4) + cross % 4 if path == 0 else 4 * (cross % 4) + (ring + 4) % 4
        return pl.ds(27 * (2 * block + path) + start, size)

    mine = (z, x)
    other = (x, z)

    def beside(path, step):
        return at(z + step, x, y) if path == 0 else at(z, x + step, y)

    def ring_copy(path, ring, cross, slot, step):
        return pltpu.make_async_remote_copy(
            term.at[c, tiles_of(path, ring, cross)], ring_slots.at[path, slot],
            ring_send.at[path, slot], ring_recv.at[path, slot],
            device_id=beside(path, step), device_id_type=MESH,
        )

    def add_ring(path, ring, cross, slots):
        tiles = tiles_of(path, ring, cross)
        value = term[c, tiles]
        for slot in slots:
            value = value + ring_slots[path, slot]
        term[c, tiles] = value

    ring = [{}, {}]
    order = [(0, 2), (1, 3)]
    for low, high in order:
        for path in range(2):
            r = mine[path]
            ring[path][low] = ring_copy(path, r + 2, low, low, 1)
            ring[path][high] = ring_copy(path, r + 2, high, high, -1)
            ring[path][low].start()
            ring[path][high].start()
    for low, high in order:
        for path in range(2):
            r = mine[path]
            ring[path][4 + high] = ring_copy(path, r + 1, high, 4 + high, 1)
            ring[path][8 + low] = ring_copy(path, r - 1, low, 8 + low, -1)
            ring[path][4 + high].start()
            ring[path][8 + low].start()

    for copy in borders:
        copy.wait()
    clear_edges(padded_up, gx, gy)
    transform_data(padded_up, dh, dl)

    for low, high in order:
        for path in range(2):
            r = mine[path]
            ring[path][low].wait_recv()
            add_ring(path, r + 1, low, (low,))
            ring[path][4 + low] = ring_copy(path, r + 1, low, 4 + low, 1)
            ring[path][4 + low].start()
            ring[path][high].wait_recv()
            add_ring(path, r - 1, high, (high,))
            ring[path][8 + high] = ring_copy(path, r - 1, high, 8 + high, -1)
            ring[path][8 + high].start()

    backward_points(dh, dl, fh, fl, product, 0, 16)

    for path in range(2):
        for slot in range(4, 12):
            ring[path][slot].wait_recv()
    for path in range(2):
        for cross in range(4):
            add_ring(path, mine[path], cross, (4 + cross, 8 + cross))

    def cross_copy(path, target, start, size, slots, index, step):
        q = other[path]
        return pltpu.make_async_remote_copy(
            term.at[c, tiles_of(path, mine[path], q + target + 4, start, size)], slots.at[pl.ds(start, size)],
            cross_send.at[path, index], cross_recv.at[path, index],
            device_id=beside(1 - path, step), device_id_type=MESH,
        )

    cross = [{}, {}]
    for path in range(2):
        plan = [
            (2, 0, 13, cross_first.at[path], 0, 1),
            (2, 13, 14, cross_first.at[path], 1, -1),
            (1, 13, 14, cross_next.at[path, 0], 2, 1),
            (-1, 0, 13, cross_next.at[path, 1], 3, -1),
        ]
        for target, start, size, slots, index, step in plan:
            cross[path][index] = cross_copy(path, target, start, size, slots, index, step)
            cross[path][index].start()
    result_of(product, filled, out)
    store = pltpu.make_async_copy(out, result, local.at[5])
    store.start()
    for path in range(2):
        for target, start, size, index, later, step in ((1, 0, 13, 0, 4, 1), (-1, 13, 14, 1, 5, -1)):
            cross[path][index].wait_recv()
            tiles = tiles_of(path, mine[path], other[path] + target + 4, start, size)
            term[c, tiles] = term[c, tiles] + cross_first[path, pl.ds(start, size)]
            slots = cross_next.at[path, 0 if step == 1 else 1]
            cross[path][later] = cross_copy(path, target, start, size, slots, later, step)
            cross[path][later].start()
    for path in range(2):
        for index in range(2, 6):
            cross[path][index].wait_recv()
        tiles = tiles_of(path, mine[path], other[path])
        final[pl.ds(27 * path, 27)] = term[c, tiles] + cross_next[path, 0] + cross_next[path, 1]

    final[pl.ds(54, 2)] = jnp.zeros((2, 8, 128), F32)
    group = lax.broadcasted_iota(jnp.int32, (8, 128), 1) // 32

    def pack(index, carry):
        parts = [final[4 * index + q] for q in range(4)]
        for target in range(4):
            moved = [
                part if q == target else pltpu.roll(part, (32 * (q - target)) % 128, 1) for q, part in enumerate(parts)
            ]
            packed[target, index] = jnp.where(
                group == 0, moved[0], jnp.where(group == 1, moved[1], jnp.where(group == 2, moved[2], moved[3]))
            )
        return carry

    lax.fori_loop(0, 14, pack, 0)
    columns = []
    for step in (2, 1, 3):
        copy = pltpu.make_async_remote_copy(
            packed.at[(y + step) % 4], packed_in.at[step - 1], column_send.at[step - 1], column_recv.at[step - 1],
            device_id=at(z, x, y + step), device_id_type=MESH,
        )
        copy.start()
        columns.append(copy)
    for copy in columns:
        copy.wait_recv()

    def unpack(index, carry):
        total = packed[y, index] + packed_in[0, index] + packed_in[1, index] + packed_in[2, index]
        for q in range(4):
            moved = total if q == 0 else pltpu.roll(total, 128 - 32 * q, 1)
            weight_grad[4 * index + q] = moved[:, :32]
        return carry

    lax.fori_loop(0, 13, unpack, 0)
    total = packed[y, 13] + packed_in[0, 13] + packed_in[1, 13] + packed_in[2, 13]
    weight_grad[52] = total[:, :32]
    weight_grad[53] = pltpu.roll(total, 96, 1)[:, :32]

    store.wait()
    for copy in core_copies.values():
        copy.wait_send()
    for path in range(2):
        for copy in ring[path].values():
            copy.wait_send()
        for copy in cross[path].values():
            copy.wait_send()
    for copy in columns:
        copy.wait_send()


def body(inputs, cotangent, weight, occupancy):
    anywhere = pl.BlockSpec(memory_space=pl.ANY)
    dma = pltpu.SemaphoreType.DMA
    result, weight_grad = pl.pallas_call(
        kernel,
        out_shape=(
            jax.ShapeDtypeStruct((8, 8, 16, 256), F32),
            jax.ShapeDtypeStruct((54, 8, 32), F32),
        ),
        in_specs=[anywhere] * 4,
        out_specs=(anywhere, pl.BlockSpec(memory_space=pltpu.VMEM)),
        scratch_shapes=[
            pltpu.VMEM((2, 864, 8, 128), F32),
            pltpu.VMEM((16, 768, 256), BF16),
            pltpu.VMEM((16, 768, 256), BF16),
            pltpu.VMEM((16, 256, 768), BF16),
            pltpu.VMEM((16, 256, 768), BF16),
            pltpu.VMEM((16, 256, 256), BF16),
            pltpu.VMEM((16, 256, 256), BF16),
            pltpu.VMEM((16, 256, 256), F32),
            pltpu.VMEM((10, 10, 16, 256), F32),
            pltpu.VMEM((10, 10, 16, 256), F32),
            pltpu.VMEM((8, 8, 16, 256), F32),
            pltpu.VMEM((8, 8, 16, 128), F32),
            pltpu.VMEM((8, 8, 16), jnp.int32),
            pltpu.VMEM((864, 8, 128), F32),
            pltpu.VMEM((2, 12, 27, 8, 128), F32),
            pltpu.VMEM((2, 27, 8, 128), F32),
            pltpu.VMEM((2, 2, 27, 8, 128), F32),
            pltpu.VMEM((4, 14, 8, 128), F32),
            pltpu.VMEM((3, 14, 8, 128), F32),
            pltpu.VMEM((8, 8, 16, 256), F32),
            pltpu.VMEM((56, 8, 128), F32),
            dma((6,)), dma((8,)), dma((8,)), dma((8,)), dma((8,)), dma((3,)), dma((3,)),
            dma((2, 12)), dma((2, 12)), dma((2, 6)), dma((2, 6)), dma((3,)), dma((3,)),
        ],
        compiler_params=pltpu.CompilerParams(
            vmem_limit_bytes=63 << 20, collective_id=0, has_side_effects=True
        ),
        name="voxels",
    )(inputs, cotangent, weight.reshape(864, 8, 256), occupancy)
    return result, weight_grad.reshape(432, 32)


def solution(mesh):
    in_specs = (P("gx", "gy", None, None), P("gx", "gy", None, None), P(), P("gx", "gy", None))
    out_specs = (P("gx", "gy", None, None), P("gx", "gy"))
    return jax.shard_map(body, mesh=mesh, in_specs=in_specs, out_specs=out_specs, check_vma=False)
```

```python
import jax, jax.numpy as jnp
from jax import lax
from jax.experimental import pallas as pl
from jax.experimental.pallas import tpu as pltpu
from jax.sharding import PartitionSpec as P

F32 = jnp.float32
BF16 = jnp.bfloat16


def split(value):
    high = value.astype(BF16)
    return high, (value - high.astype(F32)).astype(BF16)


def rows(index, size):
    return pl.ds(pl.multiple_of(index * size, size), size)


def filter_points(a, b, c):
    outer, inner = (a + c) * 0.5, b * 0.5
    return a, outer + inner, outer - inner, c


def data_points(a, b, c, d):
    return a - c, b + c, c - b, b - d


def sums_of_points(a, b, c, d):
    return a + b + c, b - c - d


def points_of_pair(a, b):
    return a, a + b, a - b, -b


def taps_of_points(a, b, c, d):
    outer = (b + c) * 0.5
    return a + outer, (b - c) * 0.5, outer + d


def both(function, grid):
    half = list(zip(*[function(*column) for column in zip(*grid)]))
    return [function(*row) for row in half]


def transform_weight(weight, high, low):
    def step(index, carry):
        grid = [
            [weight[pl.ds(pl.multiple_of((3 * a + b) * 768 + index * 16, 16), 16)] for b in range(3)]
            for a in range(3)
        ]
        points = both(filter_points, grid)
        for u in range(4):
            for v in range(4):
                top, rest = split(points[u][v])
                high[4 * u + v, rows(index, 16)] = top
                low[4 * u + v, rows(index, 16)] = rest
        return carry

    lax.fori_loop(0, 48, step, 0)


def transform_data(padded, high, low):
    def step(tile, carry):
        x, y = tile // 4, tile % 4
        grid = [[padded[2 * x + i, 2 * y + j] for j in range(4)] for i in range(4)]
        points = both(data_points, grid)
        zero = jnp.zeros((1, 256), F32)
        for u in range(4):
            for v in range(4):
                mid = points[u][v]
                down = jnp.concatenate([zero, mid[:15]], axis=0)
                up = jnp.concatenate([mid[1:], zero], axis=0)
                for place, piece in enumerate((down, mid, up)):
                    top, rest = split(piece)
                    high[4 * u + v, rows(tile, 16), 256 * place : 256 * place + 256] = top
                    low[4 * u + v, rows(tile, 16), 256 * place : 256 * place + 256] = rest
        return carry

    lax.fori_loop(0, 16, step, 0)


def dots(left_high, left_low, right_high, right_low, numbers):
    dims = (numbers, ((), ()))
    return (
        lax.dot_general(left_high, right_high, dims, preferred_element_type=F32)
        + lax.dot_general(left_low, right_high, dims, preferred_element_type=F32)
        + lax.dot_general(left_high, right_low, dims, preferred_element_type=F32)
    )


def forward(data_high, data_low, filter_high, filter_low, product):
    def step(point, carry):
        product[point] = dots(
            data_high[point], data_low[point], filter_high[point], filter_low[point], ((1,), (0,))
        )
        return carry

    lax.fori_loop(0, 16, step, 0)


def backward(data_high, data_low, filter_high, filter_low, product):
    def step(point, carry):
        u, v = point // 4, point % 4
        u = jnp.where(u == 0, 3, jnp.where(u == 3, 0, u))
        v = jnp.where(v == 0, 3, jnp.where(v == 3, 0, v))
        other = 4 * u + v
        total = None
        for place in range(3):
            lanes = slice(256 * place, 256 * place + 256)
            taps = slice(256 * (2 - place), 256 * (2 - place) + 256)
            term = dots(
                data_high[point, :, lanes],
                data_low[point, :, lanes],
                filter_high[other, taps],
                filter_low[other, taps],
                ((1,), (1,)),
            )
            total = term if total is None else total + term
        product[point] = total
        return carry

    lax.fori_loop(0, 16, step, 0)


def place_lanes(value):
    left, right = value[:, :128], value[:, 128:]
    group = lax.broadcasted_iota(jnp.int32, left.shape, 1) // 32
    left_32, right_32 = pltpu.roll(left, 96, 1), pltpu.roll(right, 32, 1)
    left_64, right_64 = pltpu.roll(left, 64, 1), pltpu.roll(right, 64, 1)
    even = jnp.where(group == 0, left, jnp.where(group == 1, left_32, jnp.where(group == 2, right_64, right_32)))
    odd = jnp.where(group == 0, left_32, jnp.where(group == 1, left_64, jnp.where(group == 2, right_32, right)))
    return jnp.concatenate([even, odd], axis=1)


def transform_filter(weight, high, low):
    def step(index, carry):
        def piece(tap):
            start = tap * 96 + index * 2
            return jnp.concatenate(
                [weight[half, pl.ds(start, 2)].reshape(16, 128) for half in range(2)], axis=1
            )

        points = both(filter_points, [[piece(3 * a + b) for b in range(3)] for a in range(3)])
        for u in range(4):
            for v in range(4):
                top, rest = split(points[u][v])
                high[4 * u + v, rows(index, 16)] = top
                low[4 * u + v, rows(index, 16)] = rest
        return carry

    lax.fori_loop(0, 48, step, 0)


def backward_points(data_high, data_low, filter_high, filter_low, product, first, last):
    def step(point, carry):
        u, v = point // 4, point % 4
        u = jnp.where(u == 0, 3, jnp.where(u == 3, 0, u))
        v = jnp.where(v == 0, 3, jnp.where(v == 3, 0, v))
        other = 4 * u + v
        total = None
        for place in range(3):
            lanes = slice(256 * place, 256 * place + 256)
            taps = slice(256 * (2 - place), 256 * (2 - place) + 256)
            term = dots(
                data_high[point, :, lanes],
                data_low[point, :, lanes],
                filter_high[other, taps],
                filter_low[other, taps],
                ((1,), (1,)),
            )
            total = term if total is None else total + term
        product[point] = total
        return carry

    lax.fori_loop(first, last, step, 0)


def twice(fill):
    return jnp.concatenate([fill, fill], axis=1)


def upstream_of(product, cotangent, filled, grid_up, up_high, up_low):
    def step(tile, carry):
        x, y = tile // 4, tile % 4
        grid = [[product[4 * u + v, rows(tile, 16)] for v in range(4)] for u in range(4)]
        sums = both(sums_of_points, grid)
        pair = []
        for i in range(2):
            line = []
            for j in range(2):
                value = sums[i][j]
                sigma = 1.0 / (1.0 + jnp.exp(-value))
                fill = twice(filled[2 * x + i, 2 * y + j])
                result = cotangent[2 * x + i, 2 * y + j] * sigma * (1.0 + value * (1.0 - sigma)) * fill
                grid_up[2 * x + i + 1, 2 * y + j + 1] = result
                line.append(place_lanes(result))
            pair.append(line)
        points = both(points_of_pair, pair)
        for u in range(4):
            for v in range(4):
                top, rest = split(points[u][v])
                up_high[4 * u + v, rows(tile, 16)] = top
                up_low[4 * u + v, rows(tile, 16)] = rest
        return carry

    lax.fori_loop(0, 16, step, 0)


def weight_points(data_high, data_low, up_high, up_low, product, place, first, count):
    lanes = slice(256 * place, 256 * place + 256)

    def step(index, carry):
        for each in range(4):
            point = first + 4 * index + each
            product[4 * index + each] = dots(
                data_high[point, :, lanes], data_low[point, :, lanes], up_high[point], up_low[point], ((0,), (0,))
            )
        return carry

    lax.fori_loop(0, count // 4, step, 0)


def store_taps(term, a, place, index, taps, add):
    for b in range(3):
        start = ((3 * a + b) * 3 + place) * 32 + 2 * index
        for half in range(2):
            value = taps[b][:, 128 * half : 128 * half + 128].reshape(2, 8, 128)
            if add:
                value = value + term[half, pl.ds(start, 2)]
            term[half, pl.ds(start, 2)] = value


def middle_taps(product, term, place):
    def step(index, carry):
        one = [product[v, rows(index, 16)] for v in range(4)]
        two = [product[4 + v, rows(index, 16)] for v in range(4)]
        outer = taps_of_points(*[(p + q) * 0.5 for p, q in zip(one, two)])
        inner = taps_of_points(*[(p - q) * 0.5 for p, q in zip(one, two)])
        store_taps(term, 0, place, index, outer, False)
        store_taps(term, 1, place, index, inner, False)
        store_taps(term, 2, place, index, outer, False)
        return carry

    lax.fori_loop(0, 16, step, 0)


def outer_taps(product, term, place, a):
    def step(index, carry):
        taps = taps_of_points(*[product[v, rows(index, 16)] for v in range(4)])
        store_taps(term, a, place, index, taps, True)
        return carry

    lax.fori_loop(0, 16, step, 0)


def result_of(product, filled, result):
    def step(tile, carry):
        x, y = tile // 4, tile % 4
        grid = [[product[4 * u + v, rows(tile, 16)] for v in range(4)] for u in range(4)]
        sums = both(sums_of_points, grid)
        for i in range(2):
            for j in range(2):
                result[2 * x + i, 2 * y + j] = sums[i][j] * twice(filled[2 * x + i, 2 * y + j])
        return carry

    lax.fori_loop(0, 16, step, 0)


def fill_of(occupancy, filled):
    same = lax.broadcasted_iota(jnp.int32, (16, 16), 0) == lax.broadcasted_iota(jnp.int32, (16, 16), 1)

    def step(x, carry):
        level = occupancy[x].astype(F32)
        for y in range(8):
            line = jnp.where(same, jnp.broadcast_to(level[y : y + 1], (16, 16)), 0.0)
            filled[x, y] = jnp.broadcast_to(jnp.sum(line, axis=1, keepdims=True), (16, 128))
        return carry

    lax.fori_loop(0, 8, step, 0)


def mask_data(padded, filled):
    def step(index, carry):
        x, y = index // 8, index % 8
        padded[x + 1, y + 1] = padded[x + 1, y + 1] * twice(filled[x, y])
        return carry

    lax.fori_loop(0, 64, step, 0)


MESH = pl.DeviceIdType.MESH
AXES = (("x", "y", "z"), ("z", "x", "y"), ("y", "z", "x"))
AROUND = [(i, j) for i in (-1, 0, 1) for j in (-1, 0, 1) if (i, j) != (0, 0)]


def strip(step):
    source = {-1: 1, 0: pl.ds(1, 8), 1: 8}[step]
    target = {-1: 9, 0: pl.ds(1, 8), 1: 0}[step]
    return source, target


def border_copies(grid, send, recv, gx, gy):
    copies = []
    for index, (i, j) in enumerate(AROUND):
        (from_x, to_x), (from_y, to_y) = strip(i), strip(j)
        copies.append(
            pltpu.make_async_remote_copy(
                grid.at[from_x, from_y],
                grid.at[to_x, to_y],
                send.at[index],
                recv.at[index],
                device_id=((gx + i + 16) % 16, (gy + j + 8) % 8),
                device_id_type=MESH,
            )
        )
    return copies


def clear_edges(grid, gx, gy):
    @pl.when(gx == 0)
    def _():
        grid[0] = jnp.zeros((10, 16, 256), F32)

    @pl.when(gx == 15)
    def _():
        grid[9] = jnp.zeros((10, 16, 256), F32)

    @pl.when(gy == 0)
    def _():
        for x in range(10):
            grid[x, 0] = jnp.zeros((16, 256), F32)

    @pl.when(gy == 7)
    def _():
        for x in range(10):
            grid[x, 9] = jnp.zeros((16, 256), F32)


def kernel(
    inputs, cotangent, weight, occupancy, result, weight_grad,
    term, fh, fl, dh, dl, eh, el, product, padded, padded_up, cot, filled, occ,
    from_core, ring_slots, cross_first, cross_next, packed, packed_in, out, final,
    local, border_send, border_recv, up_send, up_recv, core_send, core_recv,
    ring_send, ring_recv, cross_send, cross_recv, column_send, column_recv,
):
    gx, gy = lax.axis_index("gx"), lax.axis_index("gy")
    z, x, y, c = gx // 4, gx % 4, gy // 2, gy % 2

    load_inputs = pltpu.make_async_copy(inputs, padded.at[pl.ds(1, 8), pl.ds(1, 8)], local.at[0])
    load_occ = pltpu.make_async_copy(occupancy, occ, local.at[1])
    load_weight = [
        pltpu.make_async_copy(weight.at[:, :, pl.ds(128 * half, 128)], term.at[half], local.at[2 + half])
        for half in range(2)
    ]
    load_cot = pltpu.make_async_copy(cotangent, cot, local.at[4])
    for copy in (load_occ, load_inputs, *load_weight, load_cot):
        copy.start()

    place = {"z": z, "x": x, "y": y}

    def at(position):
        return (4 * position["z"] + position["x"], 2 * position["y"] + c)

    def beside(axis, step):
        return at({**place, axis: (place[axis] + step + 4) % 4})

    def target_of(a, column):
        first, second, _ = AXES[a]
        unit = 16 * a + 4 * place[first] + place[second]
        return (unit // 3, 2 * column + c), unit % 3

    def source_of(slot, index):
        unit = 3 * gx + slot
        a, high, low = unit // 16, (unit % 16) // 4, unit % 4
        position = {
            axis: sum(
                jnp.where(a == part, (high, low, index)[AXES[part].index(axis)], 0) for part in range(3)
            )
            for axis in ("z", "x", "y")
        }
        return at(position)

    partners = [((gx + i + 16) % 16, (gy + j + 8) % 8) for i, j in AROUND]
    partners += [(gx, 2 * y + 1 - c)]
    partners += [beside(axis, step) for axis in ("z", "x", "y") for step in (1, -1)]
    partners += [target_of(a, column)[0] for a in range(3) for column in range(4)]
    partners += [source_of(slot, index) for slot in range(3) for index in range(4)]
    barrier = pltpu.get_barrier_semaphore()
    for partner in partners:
        pl.semaphore_signal(barrier, inc=1, device_id=partner, device_id_type=MESH)

    load_occ.wait()
    fill_of(occ, filled)
    load_inputs.wait()
    mask_data(padded, filled)
    pl.semaphore_wait(barrier, len(partners))
    borders = border_copies(padded, border_send, border_recv, gx, gy)
    for copy in borders:
        copy.start()
    for copy in load_weight:
        copy.wait()
    transform_filter(term, fh, fl)
    for copy in borders:
        copy.wait()
    clear_edges(padded, gx, gy)
    transform_data(padded, dh, dl)
    forward(dh, dl, fh, fl, product)
    load_cot.wait()
    upstream_of(product, cot, filled, padded_up, eh, el)
    borders = border_copies(padded_up, up_send, up_recv, gx, gy)
    for copy in borders:
        copy.start()

    def to_core(a):
        taps = pl.ds(288 * a, 288)
        return pltpu.make_async_remote_copy(
            term.at[1 - c, taps], from_core.at[taps], core_send.at[a], core_recv.at[a],
            device_id=(gx, 2 * y + 1 - c), device_id_type=MESH,
        )

    def add_core(a):
        def step(index, carry):
            tiles = pl.ds(288 * a + 16 * index, 16)
            term[c, tiles] = term[c, tiles] + from_core[tiles]
            return carry

        lax.fori_loop(0, 18, step, 0)

    def axes_of(a, path):
        first, second, _ = AXES[a]
        return (first, second) if path == 0 else (second, first)

    def tiles_of(a, path, ring, cross, start=0, size=9):
        ring, cross = (ring + 4) % 4, (cross + 4) % 4
        piece = 4 * ring + cross if path == 0 else 4 * cross + ring
        return pl.ds(288 * a + 18 * piece + 9 * path + start, size)

    started = []

    def ring_copy(a, path, ring, cross, slot, step):
        which = 2 * a + path
        copy = pltpu.make_async_remote_copy(
            term.at[c, tiles_of(a, path, ring, cross)], ring_slots.at[which, slot],
            ring_send.at[which, slot], ring_recv.at[which, slot],
            device_id=beside(axes_of(a, path)[0], step), device_id_type=MESH,
        )
        copy.start()
        rings[which][slot] = copy
        started.append(copy)

    def add_ring(a, path, ring, cross, slots):
        tiles = tiles_of(a, path, ring, cross)
        value = term[c, tiles]
        for slot in slots:
            value = value + ring_slots[2 * a + path, slot]
        term[c, tiles] = value

    rings = [{} for _ in range(6)]
    crossing = [{} for _ in range(6)]
    order = ((0, 2), (1, 3))

    def ring_first(a):
        for low, high in order:
            for path in range(2):
                r = place[axes_of(a, path)[0]]
                ring_copy(a, path, r + 2, low, low, 1)
                ring_copy(a, path, r + 2, high, high, -1)
        for low, high in order:
            for path in range(2):
                r = place[axes_of(a, path)[0]]
                ring_copy(a, path, r + 1, high, 4 + high, 1)
                ring_copy(a, path, r - 1, low, 8 + low, -1)

    def ring_second(a):
        for low, high in order:
            for path in range(2):
                r = place[axes_of(a, path)[0]]
                rings[2 * a + path][low].wait_recv()
                add_ring(a, path, r + 1, low, (low,))
                ring_copy(a, path, r + 1, low, 4 + low, 1)
                rings[2 * a + path][high].wait_recv()
                add_ring(a, path, r - 1, high, (high,))
                ring_copy(a, path, r - 1, high, 8 + high, -1)

    def cross_copy(a, path, target, start, size, slots, index, step):
        which, (along, across) = 2 * a + path, axes_of(a, path)
        copy = pltpu.make_async_remote_copy(
            term.at[c, tiles_of(a, path, place[along], place[across] + target, start, size)], slots.at[pl.ds(start, size)],
            cross_send.at[which, index], cross_recv.at[which, index],
            device_id=beside(across, step), device_id_type=MESH,
        )
        copy.start()
        crossing[which][index] = copy
        started.append(copy)

    def ring_last(a):
        for path in range(2):
            for slot in range(4, 12):
                rings[2 * a + path][slot].wait_recv()
            for cross in range(4):
                add_ring(a, path, place[axes_of(a, path)[0]], cross, (4 + cross, 8 + cross))
        for path in range(2):
            which = 2 * a + path
            cross_copy(a, path, 2, 0, 4, cross_first.at[which], 0, 1)
            cross_copy(a, path, 2, 4, 5, cross_first.at[which], 1, -1)
        for path in range(2):
            which = 2 * a + path
            cross_copy(a, path, 1, 4, 5, cross_next.at[which, 0], 2, 1)
            cross_copy(a, path, -1, 0, 4, cross_next.at[which, 1], 3, -1)

    def cross_second(a):
        for path in range(2):
            which, (along, across) = 2 * a + path, axes_of(a, path)
            for target, start, size, index, step in ((1, 0, 4, 0, 1), (-1, 4, 5, 1, -1)):
                crossing[which][index].wait_recv()
                tiles = tiles_of(a, path, place[along], place[across] + target, start, size)
                term[c, tiles] = term[c, tiles] + cross_first[which, pl.ds(start, size)]
                cross_copy(a, path, target, start, size, cross_next.at[which, index], 4 + index, step)

    group = lax.broadcasted_iota(jnp.int32, (8, 128), 1) // 32
    columns = []

    def column_copy(a, column):
        target, slot = target_of(a, column)
        index = place[AXES[a][2]]
        here = jnp.logical_and(target[0] == gx, column == y)
        local_copy = pltpu.make_async_copy(
            packed.at[a, column], packed_in.at[slot, index], column_recv.at[slot, index]
        )
        copy = pltpu.make_async_remote_copy(
            packed.at[a, column], packed_in.at[slot, index], column_send.at[a, column], column_recv.at[slot, index],
            device_id=target, device_id_type=MESH,
        )
        pl.when(here)(local_copy.start)
        pl.when(jnp.logical_not(here))(copy.start)
        columns.append((here, copy))

    def cross_last(a):
        for path in range(2):
            which = 2 * a + path
            for index in range(2, 6):
                crossing[which][index].wait_recv()
            along, across = axes_of(a, path)
            tiles = tiles_of(a, path, place[along], place[across])
            final[pl.ds(9 * path, 9)] = term[c, tiles] + cross_next[which, 0] + cross_next[which, 1]
        for index in range(5):
            parts = [final[min(4 * index + q, 17)] for q in range(4)]
            for column in range(4):
                moved = [
                    part if q == column else pltpu.roll(part, (32 * (q - column)) % 128, 1)
                    for q, part in enumerate(parts)
                ]
                packed[a, column, index] = jnp.where(
                    group == 0, moved[0], jnp.where(group == 1, moved[1], jnp.where(group == 2, moved[2], moved[3]))
                )
        for column in range(4):
            column_copy(a, column)

    core_copies = {}

    def weight_part(a, first, count):
        for place_z in range(3):
            weight_points(dh, dl, eh, el, product, place_z, first, count)
            if a == 1:
                middle_taps(product, term, place_z)
            else:
                outer_taps(product, term, place_z, a)
        core_copies[a] = to_core(a)
        core_copies[a].start()

    def core_sum(a):
        core_copies[a].wait_recv()
        add_core(a)

    weight_part(1, 4, 8)
    weight_part(0, 0, 4)
    core_sum(1)
    ring_first(1)
    weight_part(2, 12, 4)
    core_sum(0)
    ring_first(0)
    for copy in borders:
        copy.wait()
    clear_edges(padded_up, gx, gy)
    transform_data(padded_up, dh, dl)
    core_sum(2)
    ring_first(2)
    ring_second(1)
    ring_second(0)
    backward_points(dh, dl, fh, fl, product, 0, 4)
    ring_last(1)
    ring_second(2)
    backward_points(dh, dl, fh, fl, product, 4, 8)
    ring_last(0)
    cross_second(1)
    backward_points(dh, dl, fh, fl, product, 8, 12)
    ring_last(2)
    cross_second(0)
    cross_last(1)
    backward_points(dh, dl, fh, fl, product, 12, 16)
    result_of(product, filled, out)
    store = pltpu.make_async_copy(out, result, local.at[5])
    store.start()
    cross_second(2)
    cross_last(0)
    cross_last(2)
    for slot in range(3):
        for index in range(4):
            pltpu.make_async_copy(
                packed.at[0, 0], packed_in.at[slot, index], column_recv.at[slot, index]
            ).wait()
    for slot in range(3):
        for index in range(5):
            total = (packed_in[slot, 0, index] + packed_in[slot, 1, index]) + (
                packed_in[slot, 2, index] + packed_in[slot, 3, index]
            )
            for q in range(4 if index < 4 else 2):
                final[18 * slot + 4 * index + q] = total if q == 0 else pltpu.roll(total, 128 - 32 * q, 1)
    weight_grad[...] = final[...].reshape(448, 128).T[:32, :432]
    store.wait()
    for copy in (*core_copies.values(), *started):
        copy.wait_send()
    for here, copy in columns:
        pl.when(jnp.logical_not(here))(copy.wait_send)


def body(inputs, cotangent, weight, occupancy):
    anywhere = pl.BlockSpec(memory_space=pl.ANY)
    dma = pltpu.SemaphoreType.DMA
    result, weight_grad = pl.pallas_call(
        kernel,
        out_shape=(
            jax.ShapeDtypeStruct((8, 8, 16, 256), F32),
            jax.ShapeDtypeStruct((32, 432), F32),
        ),
        in_specs=[anywhere] * 4,
        out_specs=(anywhere, pl.BlockSpec(memory_space=pltpu.VMEM)),
        scratch_shapes=[
            pltpu.VMEM((2, 864, 8, 128), F32),
            pltpu.VMEM((16, 768, 256), BF16),
            pltpu.VMEM((16, 768, 256), BF16),
            pltpu.VMEM((16, 256, 768), BF16),
            pltpu.VMEM((16, 256, 768), BF16),
            pltpu.VMEM((16, 256, 256), BF16),
            pltpu.VMEM((16, 256, 256), BF16),
            pltpu.VMEM((16, 256, 256), F32),
            pltpu.VMEM((10, 10, 16, 256), F32),
            pltpu.VMEM((10, 10, 16, 256), F32),
            pltpu.VMEM((8, 8, 16, 256), F32),
            pltpu.VMEM((8, 8, 16, 128), F32),
            pltpu.VMEM((8, 8, 16), jnp.int32),
            pltpu.VMEM((864, 8, 128), F32),
            pltpu.VMEM((6, 12, 9, 8, 128), F32),
            pltpu.VMEM((6, 9, 8, 128), F32),
            pltpu.VMEM((6, 2, 9, 8, 128), F32),
            pltpu.VMEM((3, 4, 5, 8, 128), F32),
            pltpu.VMEM((3, 4, 5, 8, 128), F32),
            pltpu.VMEM((8, 8, 16, 256), F32),
            pltpu.VMEM((56, 8, 128), F32),
            dma((6,)), dma((8,)), dma((8,)), dma((8,)), dma((8,)), dma((3,)), dma((3,)),
            dma((6, 12)), dma((6, 12)), dma((6, 6)), dma((6, 6)), dma((3, 4)), dma((3, 4)),
        ],
        compiler_params=pltpu.CompilerParams(
            vmem_limit_bytes=63 << 20, collective_id=0, has_side_effects=True
        ),
        name="voxels",
    )(inputs, cotangent, weight.reshape(864, 8, 256), occupancy)
    return result, weight_grad.T


def solution(mesh):
    in_specs = (P("gx", "gy", None, None), P("gx", "gy", None, None), P(), P("gx", "gy", None))
    out_specs = (P("gx", "gy", None, None), P("gx", "gy"))
    return jax.shard_map(body, mesh=mesh, in_specs=in_specs, out_specs=out_specs, check_vma=False)
```

```python
import jax, jax.numpy as jnp
from jax import lax
from jax.experimental import pallas as pl
from jax.experimental.pallas import tpu as pltpu
from jax.sharding import PartitionSpec as P

F32 = jnp.float32
BF16 = jnp.bfloat16


def split(value):
    high = value.astype(BF16)
    return high, (value - high.astype(F32)).astype(BF16)


def rows(index, size):
    return pl.ds(pl.multiple_of(index * size, size), size)


def filter_points(a, b, c):
    outer, inner = (a + c) * 0.5, b * 0.5
    return a, outer + inner, outer - inner, c


def data_points(a, b, c, d):
    return a - c, b + c, c - b, b - d


def sums_of_points(a, b, c, d):
    return a + b + c, b - c - d


def points_of_pair(a, b):
    return a, a + b, a - b, -b


def taps_of_points(a, b, c, d):
    outer = (b + c) * 0.5
    return a + outer, (b - c) * 0.5, outer + d


def both(function, grid):
    half = list(zip(*[function(*column) for column in zip(*grid)]))
    return [function(*row) for row in half]


def data_tiles(padded, high, low, first, last):
    def step(tile, carry):
        x, y = tile // 4, tile % 4
        grid = [[padded[2 * x + i, 2 * y + j] for j in range(4)] for i in range(4)]
        points = both(data_points, grid)
        zero = jnp.zeros((1, 256), F32)
        for u in range(4):
            for v in range(4):
                mid = points[u][v]
                down = jnp.concatenate([zero, mid[:15]], axis=0)
                up = jnp.concatenate([mid[1:], zero], axis=0)
                for place, piece in enumerate((down, mid, up)):
                    top, rest = split(piece)
                    high[4 * u + v, rows(tile, 16), 256 * place : 256 * place + 256] = top
                    low[4 * u + v, rows(tile, 16), 256 * place : 256 * place + 256] = rest
        return carry

    lax.fori_loop(first, last, step, 0)


def dots(left_high, left_low, right_high, right_low, numbers):
    dims = (numbers, ((), ()))
    return (
        lax.dot_general(left_high, right_high, dims, preferred_element_type=F32)
        + lax.dot_general(left_low, right_high, dims, preferred_element_type=F32)
        + lax.dot_general(left_high, right_low, dims, preferred_element_type=F32)
    )


def forward(data_high, data_low, filter_high, filter_low, product):
    def step(point, carry):
        product[point] = dots(
            data_high[point], data_low[point], filter_high[point], filter_low[point], ((1,), (0,))
        )
        return carry

    lax.fori_loop(0, 16, step, 0)


def place_lanes(value):
    left, right = value[:, :128], value[:, 128:]
    group = lax.broadcasted_iota(jnp.int32, left.shape, 1) // 32
    left_32, right_32 = pltpu.roll(left, 96, 1), pltpu.roll(right, 32, 1)
    left_64, right_64 = pltpu.roll(left, 64, 1), pltpu.roll(right, 64, 1)
    even = jnp.where(group == 0, left, jnp.where(group == 1, left_32, jnp.where(group == 2, right_64, right_32)))
    odd = jnp.where(group == 0, left_32, jnp.where(group == 1, left_64, jnp.where(group == 2, right_32, right)))
    return jnp.concatenate([even, odd], axis=1)


def transform_filter(weight, high, low):
    def step(index, carry):
        def piece(tap):
            start = tap * 96 + index * 2
            return jnp.concatenate(
                [weight[half, pl.ds(start, 2)].reshape(16, 128) for half in range(2)], axis=1
            )

        points = both(filter_points, [[piece(3 * a + b) for b in range(3)] for a in range(3)])
        for u in range(4):
            for v in range(4):
                top, rest = split(points[u][v])
                high[4 * u + v, rows(index, 16)] = top
                low[4 * u + v, rows(index, 16)] = rest
        return carry

    lax.fori_loop(0, 48, step, 0)


def backward_points(data_high, data_low, filter_high, filter_low, product, first, last):
    def step(point, carry):
        u, v = point // 4, point % 4
        u = jnp.where(u == 0, 3, jnp.where(u == 3, 0, u))
        v = jnp.where(v == 0, 3, jnp.where(v == 3, 0, v))
        other = 4 * u + v
        total = None
        for place in range(3):
            lanes = slice(256 * place, 256 * place + 256)
            taps = slice(256 * (2 - place), 256 * (2 - place) + 256)
            term = dots(
                data_high[point, :, lanes],
                data_low[point, :, lanes],
                filter_high[other, taps],
                filter_low[other, taps],
                ((1,), (1,)),
            )
            total = term if total is None else total + term
        product[point] = total
        return carry

    lax.fori_loop(first, last, step, 0)


def twice(fill):
    return jnp.concatenate([fill, fill], axis=1)


def upstream_of(product, cotangent, filled, grid_up, up_high, up_low):
    def step(tile, carry):
        x, y = tile // 4, tile % 4
        grid = [[product[4 * u + v, rows(tile, 16)] for v in range(4)] for u in range(4)]
        sums = both(sums_of_points, grid)
        pair = []
        for i in range(2):
            line = []
            for j in range(2):
                value = sums[i][j]
                sigma = 1.0 / (1.0 + jnp.exp(-value))
                fill = twice(filled[2 * x + i, 2 * y + j])
                result = cotangent[2 * x + i, 2 * y + j] * sigma * (1.0 + value * (1.0 - sigma)) * fill
                grid_up[2 * x + i + 1, 2 * y + j + 1] = result
                line.append(place_lanes(result))
            pair.append(line)
        points = both(points_of_pair, pair)
        for u in range(4):
            for v in range(4):
                top, rest = split(points[u][v])
                up_high[4 * u + v, rows(tile, 16)] = top
                up_low[4 * u + v, rows(tile, 16)] = rest
        return carry

    lax.fori_loop(0, 16, step, 0)


def weight_points(data_high, data_low, up_high, up_low, product, place, first, count):
    lanes = slice(256 * place, 256 * place + 256)

    def step(index, carry):
        for each in range(4):
            point = first + 4 * index + each
            product[4 * index + each] = dots(
                data_high[point, :, lanes], data_low[point, :, lanes], up_high[point], up_low[point], ((0,), (0,))
            )
        return carry

    lax.fori_loop(0, count // 4, step, 0)


def store_taps(term, a, place, index, taps, add):
    for b in range(3):
        start = ((3 * a + b) * 3 + place) * 32 + 2 * index
        for half in range(2):
            value = taps[b][:, 128 * half : 128 * half + 128].reshape(2, 8, 128)
            if add:
                value = value + term[half, pl.ds(start, 2)]
            term[half, pl.ds(start, 2)] = value


def middle_taps(product, term, place):
    def step(index, carry):
        one = [product[v, rows(index, 16)] for v in range(4)]
        two = [product[4 + v, rows(index, 16)] for v in range(4)]
        outer = taps_of_points(*[(p + q) * 0.5 for p, q in zip(one, two)])
        inner = taps_of_points(*[(p - q) * 0.5 for p, q in zip(one, two)])
        store_taps(term, 0, place, index, outer, False)
        store_taps(term, 1, place, index, inner, False)
        store_taps(term, 2, place, index, outer, False)
        return carry

    lax.fori_loop(0, 16, step, 0)


def outer_taps(product, term, place, a):
    def step(index, carry):
        taps = taps_of_points(*[product[v, rows(index, 16)] for v in range(4)])
        store_taps(term, a, place, index, taps, True)
        return carry

    lax.fori_loop(0, 16, step, 0)


def result_of(product, filled, result):
    def step(tile, carry):
        x, y = tile // 4, tile % 4
        grid = [[product[4 * u + v, rows(tile, 16)] for v in range(4)] for u in range(4)]
        sums = both(sums_of_points, grid)
        for i in range(2):
            for j in range(2):
                result[2 * x + i, 2 * y + j] = sums[i][j] * twice(filled[2 * x + i, 2 * y + j])
        return carry

    lax.fori_loop(0, 16, step, 0)


def fill_of(occupancy, filled):
    same = lax.broadcasted_iota(jnp.int32, (16, 16), 0) == lax.broadcasted_iota(jnp.int32, (16, 16), 1)

    def step(x, carry):
        level = occupancy[x].astype(F32)
        for y in range(8):
            line = jnp.where(same, jnp.broadcast_to(level[y : y + 1], (16, 16)), 0.0)
            filled[x, y] = jnp.broadcast_to(jnp.sum(line, axis=1, keepdims=True), (16, 128))
        return carry

    lax.fori_loop(0, 8, step, 0)


def mask_data(padded, filled):
    def step(index, carry):
        x, y = index // 8, index % 8
        padded[x + 1, y + 1] = padded[x + 1, y + 1] * twice(filled[x, y])
        return carry

    lax.fori_loop(0, 64, step, 0)


MESH = pl.DeviceIdType.MESH
AXES = (("x", "y", "z"), ("z", "x", "y"), ("y", "z", "x"))
AROUND = [(i, j) for i in (-1, 0, 1) for j in (-1, 0, 1) if (i, j) != (0, 0)]


def strip(step):
    source = {-1: 1, 0: pl.ds(1, 8), 1: 8}[step]
    target = {-1: 9, 0: pl.ds(1, 8), 1: 0}[step]
    return source, target


def border_copies(grid, send, recv, gx, gy):
    copies = []
    for index, (i, j) in enumerate(AROUND):
        (from_x, to_x), (from_y, to_y) = strip(i), strip(j)
        copies.append(
            pltpu.make_async_remote_copy(
                grid.at[from_x, from_y],
                grid.at[to_x, to_y],
                send.at[index],
                recv.at[index],
                device_id=((gx + i + 16) % 16, (gy + j + 8) % 8),
                device_id_type=MESH,
            )
        )
    return copies


def take_sides(grid, copies, gy):
    for (i, _), copy in zip(AROUND, copies):
        if i == 0:
            copy.wait()

    def clear(y):
        for x in range(1, 9):
            grid[x, y] = jnp.zeros((16, 256), F32)

    pl.when(gy == 0)(lambda: clear(0))
    pl.when(gy == 7)(lambda: clear(9))


def take_rest(grid, copies, gx, gy):
    for (i, _), copy in zip(AROUND, copies):
        if i != 0:
            copy.wait()

    def clear(x, y):
        grid[x, y] = jnp.zeros((16, 256), F32)

    def clear_row(x):
        grid[x] = jnp.zeros((10, 16, 256), F32)

    def clear_corners(y):
        clear(0, y)
        clear(9, y)

    pl.when(gx == 0)(lambda: clear_row(0))
    pl.when(gx == 15)(lambda: clear_row(9))
    pl.when(gy == 0)(lambda: clear_corners(0))
    pl.when(gy == 7)(lambda: clear_corners(9))


def kernel(
    inputs, cotangent, weight, occupancy, result, weight_grad,
    term, fh, fl, dh, dl, eh, el, product, padded, padded_up, cot, filled, occ,
    from_core, ring_slots, cross_first, cross_next, packed, packed_in, final,
    local, border_send, border_recv, up_send, up_recv, core_send, core_recv,
    ring_send, ring_recv, cross_send, cross_recv, column_send, column_recv,
):
    gx, gy = lax.axis_index("gx"), lax.axis_index("gy")
    z, x, y, c = gx // 4, gx % 4, gy // 2, gy % 2

    load_inputs = pltpu.make_async_copy(inputs, padded.at[pl.ds(1, 8), pl.ds(1, 8)], local.at[0])
    load_occ = pltpu.make_async_copy(occupancy, occ, local.at[1])
    load_weight = [
        pltpu.make_async_copy(weight.at[:, :, pl.ds(128 * half, 128)], term.at[half], local.at[2 + half])
        for half in range(2)
    ]
    load_cot = pltpu.make_async_copy(cotangent, cot, local.at[4])
    for copy in (load_occ, load_inputs, *load_weight, load_cot):
        copy.start()

    place = {"z": z, "x": x, "y": y}

    def at(position):
        return (4 * position["z"] + position["x"], 2 * position["y"] + c)

    def beside(axis, step):
        return at({**place, axis: (place[axis] + step + 4) % 4})

    def target_of(a, column):
        first, second, _ = AXES[a]
        unit = 16 * a + 4 * place[first] + place[second]
        return (unit // 3, 2 * column + c), unit % 3

    def source_of(slot, index):
        unit = 3 * gx + slot
        a, high, low = unit // 16, (unit % 16) // 4, unit % 4
        position = {
            axis: sum(
                jnp.where(a == part, (high, low, index)[AXES[part].index(axis)], 0) for part in range(3)
            )
            for axis in ("z", "x", "y")
        }
        return at(position)

    partners = [((gx + i + 16) % 16, (gy + j + 8) % 8) for i, j in AROUND]
    partners += [(gx, 2 * y + 1 - c)]
    partners += [beside(axis, step) for axis in ("z", "x", "y") for step in (1, -1)]
    partners += [target_of(a, column)[0] for a in range(3) for column in range(4)]
    partners += [source_of(slot, index) for slot in range(3) for index in range(4)]
    barrier = pltpu.get_barrier_semaphore()
    for partner in partners:
        pl.semaphore_signal(barrier, inc=1, device_id=partner, device_id_type=MESH)

    load_occ.wait()
    fill_of(occ, filled)
    load_inputs.wait()
    mask_data(padded, filled)
    pl.semaphore_wait(barrier, len(partners))
    borders = border_copies(padded, border_send, border_recv, gx, gy)
    for copy in borders:
        copy.start()
    for copy in load_weight:
        copy.wait()
    transform_filter(term, fh, fl)
    take_sides(padded, borders, gy)
    data_tiles(padded, dh, dl, 4, 12)
    take_rest(padded, borders, gx, gy)
    data_tiles(padded, dh, dl, 0, 4)
    data_tiles(padded, dh, dl, 12, 16)
    forward(dh, dl, fh, fl, product)
    load_cot.wait()
    upstream_of(product, cot, filled, padded_up, eh, el)
    borders = border_copies(padded_up, up_send, up_recv, gx, gy)
    for copy in borders:
        copy.start()

    def to_core(a, place_z, b):
        index = 9 * a + 3 * place_z + b
        taps = pl.ds(((3 * a + b) * 3 + place_z) * 32, 32)
        return pltpu.make_async_remote_copy(
            term.at[1 - c, taps], from_core.at[taps], core_send.at[index], core_recv.at[index],
            device_id=(gx, 2 * y + 1 - c), device_id_type=MESH,
        )

    def add_core(a):
        def step(index, carry):
            tiles = pl.ds(288 * a + 16 * index, 16)
            term[c, tiles] = term[c, tiles] + from_core[tiles]
            return carry

        lax.fori_loop(0, 18, step, 0)

    def axes_of(a, path):
        first, second, _ = AXES[a]
        return (first, second) if path == 0 else (second, first)

    def tiles_of(a, path, ring, cross, start=0, size=9):
        ring, cross = (ring + 4) % 4, (cross + 4) % 4
        piece = 4 * ring + cross if path == 0 else 4 * cross + ring
        return pl.ds(288 * a + 18 * piece + 9 * path + start, size)

    started = []

    def ring_copy(a, path, ring, cross, slot, step):
        which = 2 * a + path
        copy = pltpu.make_async_remote_copy(
            term.at[c, tiles_of(a, path, ring, cross)], ring_slots.at[which, slot],
            ring_send.at[which, slot], ring_recv.at[which, slot],
            device_id=beside(axes_of(a, path)[0], step), device_id_type=MESH,
        )
        copy.start()
        rings[which][slot] = copy
        started.append(copy)

    def add_ring(a, path, ring, cross, slots):
        tiles = tiles_of(a, path, ring, cross)
        value = term[c, tiles]
        for slot in slots:
            value = value + ring_slots[2 * a + path, slot]
        term[c, tiles] = value

    rings = [{} for _ in range(6)]
    crossing = [{} for _ in range(6)]
    order = ((0, 2), (1, 3))

    def ring_first(a):
        for low, high in order:
            for path in range(2):
                r = place[axes_of(a, path)[0]]
                ring_copy(a, path, r + 2, low, low, 1)
                ring_copy(a, path, r + 2, high, high, -1)
        for low, high in order:
            for path in range(2):
                r = place[axes_of(a, path)[0]]
                ring_copy(a, path, r + 1, high, 4 + high, 1)
                ring_copy(a, path, r - 1, low, 8 + low, -1)

    def ring_second(a):
        for low, high in order:
            for path in range(2):
                r = place[axes_of(a, path)[0]]
                rings[2 * a + path][low].wait_recv()
                add_ring(a, path, r + 1, low, (low,))
                ring_copy(a, path, r + 1, low, 4 + low, 1)
                rings[2 * a + path][high].wait_recv()
                add_ring(a, path, r - 1, high, (high,))
                ring_copy(a, path, r - 1, high, 8 + high, -1)

    def cross_copy(a, path, target, start, size, slots, index, step):
        which, (along, across) = 2 * a + path, axes_of(a, path)
        copy = pltpu.make_async_remote_copy(
            term.at[c, tiles_of(a, path, place[along], place[across] + target, start, size)], slots.at[pl.ds(start, size)],
            cross_send.at[which, index], cross_recv.at[which, index],
            device_id=beside(across, step), device_id_type=MESH,
        )
        copy.start()
        crossing[which][index] = copy
        started.append(copy)

    def ring_last(a):
        for path in range(2):
            for slot in range(4, 12):
                rings[2 * a + path][slot].wait_recv()
            for cross in range(4):
                add_ring(a, path, place[axes_of(a, path)[0]], cross, (4 + cross, 8 + cross))
        for path in range(2):
            which = 2 * a + path
            cross_copy(a, path, 2, 0, 4, cross_first.at[which], 0, 1)
            cross_copy(a, path, 2, 4, 5, cross_first.at[which], 1, -1)
        for path in range(2):
            which = 2 * a + path
            cross_copy(a, path, 1, 4, 5, cross_next.at[which, 0], 2, 1)
            cross_copy(a, path, -1, 0, 4, cross_next.at[which, 1], 3, -1)

    def cross_second(a):
        for path in range(2):
            which, (along, across) = 2 * a + path, axes_of(a, path)
            for target, start, size, index, step in ((1, 0, 4, 0, 1), (-1, 4, 5, 1, -1)):
                crossing[which][index].wait_recv()
                tiles = tiles_of(a, path, place[along], place[across] + target, start, size)
                term[c, tiles] = term[c, tiles] + cross_first[which, pl.ds(start, size)]
                cross_copy(a, path, target, start, size, cross_next.at[which, index], 4 + index, step)

    group = lax.broadcasted_iota(jnp.int32, (8, 128), 1) // 32
    columns = []

    def column_copy(a, column):
        target, slot = target_of(a, column)
        index = place[AXES[a][2]]
        here = jnp.logical_and(target[0] == gx, column == y)
        local_copy = pltpu.make_async_copy(
            packed.at[a, column], packed_in.at[slot, index], column_recv.at[slot, index]
        )
        copy = pltpu.make_async_remote_copy(
            packed.at[a, column], packed_in.at[slot, index], column_send.at[a, column], column_recv.at[slot, index],
            device_id=target, device_id_type=MESH,
        )
        pl.when(here)(local_copy.start)
        pl.when(jnp.logical_not(here))(copy.start)
        columns.append((here, copy))

    def cross_last(a):
        for path in range(2):
            which = 2 * a + path
            for index in range(2, 6):
                crossing[which][index].wait_recv()
            along, across = axes_of(a, path)
            tiles = tiles_of(a, path, place[along], place[across])
            final[pl.ds(9 * path, 9)] = term[c, tiles] + cross_next[which, 0] + cross_next[which, 1]
        for index in range(5):
            parts = [final[min(4 * index + q, 17)] for q in range(4)]
            for column in range(4):
                moved = [
                    part if q == column else pltpu.roll(part, (32 * (q - column)) % 128, 1)
                    for q, part in enumerate(parts)
                ]
                packed[a, column, index] = jnp.where(
                    group == 0, moved[0], jnp.where(group == 1, moved[1], jnp.where(group == 2, moved[2], moved[3]))
                )
        for column in range(4):
            column_copy(a, column)

    core_copies = {}

    def weight_part(a, first, count, places=(0, 1, 2)):
        for place_z in places:
            weight_points(dh, dl, eh, el, product, place_z, first, count)
            if a == 1:
                middle_taps(product, term, place_z)
            else:
                outer_taps(product, term, place_z, a)
            for b in range(3):
                copy = to_core(a, place_z, b)
                copy.start()
                core_copies.setdefault(a, []).append(copy)

    def core_sum(a):
        for copy in core_copies[a]:
            copy.wait_recv()
        add_core(a)

    def points(first, last):
        backward_points(dh, dl, fh, fl, product, first, last)

    weight_part(1, 4, 8)
    weight_part(0, 0, 4, (0,))
    core_sum(1)
    ring_first(1)
    weight_part(0, 0, 4, (1, 2))
    weight_part(2, 12, 4, (0,))
    core_sum(0)
    ring_first(0)
    weight_part(2, 12, 4, (1, 2))
    ring_second(1)
    take_sides(padded_up, borders, gy)
    take_rest(padded_up, borders, gx, gy)
    data_tiles(padded_up, dh, dl, 0, 5)
    core_sum(2)
    ring_first(2)
    data_tiles(padded_up, dh, dl, 5, 16)
    ring_second(0)
    points(0, 2)
    ring_last(1)
    points(2, 4)
    ring_second(2)
    points(4, 7)
    ring_last(0)
    cross_second(1)
    points(7, 10)
    ring_last(2)
    cross_last(1)
    points(10, 12)
    cross_second(0)
    points(12, 14)
    cross_second(2)
    points(14, 16)
    result_of(product, filled, result)
    cross_last(0)
    cross_last(2)
    for slot in range(3):
        for index in range(4):
            pltpu.make_async_copy(
                packed.at[0, 0], packed_in.at[slot, index], column_recv.at[slot, index]
            ).wait()
    for slot in range(3):
        for index in range(5):
            total = (packed_in[slot, 0, index] + packed_in[slot, 1, index]) + (
                packed_in[slot, 2, index] + packed_in[slot, 3, index]
            )
            for q in range(4 if index < 4 else 2):
                final[18 * slot + 4 * index + q] = total if q == 0 else pltpu.roll(total, 128 - 32 * q, 1)
    weight_grad[...] = final[...].reshape(448, 128).T[:32, :432]
    for copy in (*core_copies[0], *core_copies[1], *core_copies[2], *started):
        copy.wait_send()
    for here, copy in columns:
        pl.when(jnp.logical_not(here))(copy.wait_send)


def body(inputs, cotangent, weight, occupancy):
    anywhere = pl.BlockSpec(memory_space=pl.ANY)
    dma = pltpu.SemaphoreType.DMA
    result, weight_grad = pl.pallas_call(
        kernel,
        out_shape=(
            pltpu.VMEM((8, 8, 16, 256), F32),
            pltpu.VMEM((32, 432), F32),
        ),
        in_specs=[anywhere] * 4,
        out_specs=(pl.BlockSpec(memory_space=pltpu.VMEM),) * 2,
        scratch_shapes=[
            pltpu.VMEM((2, 864, 8, 128), F32),
            pltpu.VMEM((16, 768, 256), BF16),
            pltpu.VMEM((16, 768, 256), BF16),
            pltpu.VMEM((16, 256, 768), BF16),
            pltpu.VMEM((16, 256, 768), BF16),
            pltpu.VMEM((16, 256, 256), BF16),
            pltpu.VMEM((16, 256, 256), BF16),
            pltpu.VMEM((16, 256, 256), F32),
            pltpu.VMEM((10, 10, 16, 256), F32),
            pltpu.VMEM((10, 10, 16, 256), F32),
            pltpu.VMEM((8, 8, 16, 256), F32),
            pltpu.VMEM((8, 8, 16, 128), F32),
            pltpu.VMEM((8, 8, 16), jnp.int32),
            pltpu.VMEM((864, 8, 128), F32),
            pltpu.VMEM((6, 12, 9, 8, 128), F32),
            pltpu.VMEM((6, 9, 8, 128), F32),
            pltpu.VMEM((6, 2, 9, 8, 128), F32),
            pltpu.VMEM((3, 4, 5, 8, 128), F32),
            pltpu.VMEM((3, 4, 5, 8, 128), F32),
            pltpu.VMEM((56, 8, 128), F32),
            dma((5,)), dma((8,)), dma((8,)), dma((8,)), dma((8,)), dma((27,)), dma((27,)),
            dma((6, 12)), dma((6, 12)), dma((6, 6)), dma((6, 6)), dma((3, 4)), dma((3, 4)),
        ],
        compiler_params=pltpu.CompilerParams(
            vmem_limit_bytes=56 << 20, collective_id=0, has_side_effects=True
        ),
        name="voxels",
    )(inputs, cotangent, weight.reshape(864, 8, 256), occupancy)
    return result, weight_grad.T


def solution(mesh):
    in_specs = (P("gx", "gy", None, None), P("gx", "gy", None, None), P(), P("gx", "gy", None))
    out_specs = (P("gx", "gy", None, None), P("gx", "gy"))
    return jax.shard_map(body, mesh=mesh, in_specs=in_specs, out_specs=out_specs, check_vma=False)
```

```python
import jax, jax.numpy as jnp
from jax import lax
from jax.experimental import pallas as pl
from jax.experimental.pallas import tpu as pltpu
from jax.sharding import PartitionSpec as P

F32 = jnp.float32
BF16 = jnp.bfloat16


def split(value):
    high = value.astype(BF16)
    return high, (value - high.astype(F32)).astype(BF16)


def rows(index, size):
    return pl.ds(pl.multiple_of(index * size, size), size)


def filter_points(a, b, c):
    outer, inner = (a + c) * 0.5, b * 0.5
    return a, outer + inner, outer - inner, c


def data_points(a, b, c, d):
    return a - c, b + c, c - b, b - d


def sums_of_points(a, b, c, d):
    return a + b + c, b - c - d


def points_of_pair(a, b):
    return a, a + b, a - b, -b


def taps_of_points(a, b, c, d):
    outer = (b + c) * 0.5
    return a + outer, (b - c) * 0.5, outer + d


def both(function, grid):
    half = list(zip(*[function(*column) for column in zip(*grid)]))
    return [function(*row) for row in half]


def data_tiles(padded, high, low, first, last):
    def step(tile, carry):
        x, y = tile // 4, tile % 4
        grid = [[padded[2 * x + i, 2 * y + j] for j in range(4)] for i in range(4)]
        points = both(data_points, grid)
        zero = jnp.zeros((1, 256), F32)
        for u in range(4):
            for v in range(4):
                mid = points[u][v]
                down = jnp.concatenate([zero, mid[:15]], axis=0)
                up = jnp.concatenate([mid[1:], zero], axis=0)
                for place, piece in enumerate((down, mid, up)):
                    top, rest = split(piece)
                    high[4 * u + v, rows(tile, 16), 256 * place : 256 * place + 256] = top
                    low[4 * u + v, rows(tile, 16), 256 * place : 256 * place + 256] = rest
        return carry

    lax.fori_loop(first, last, step, 0)


def dots(left_high, left_low, right_high, right_low, numbers):
    dims = (numbers, ((), ()))
    return (
        lax.dot_general(left_high, right_high, dims, preferred_element_type=F32)
        + lax.dot_general(left_low, right_high, dims, preferred_element_type=F32)
        + lax.dot_general(left_high, right_low, dims, preferred_element_type=F32)
    )


def forward(data_high, data_low, filter_high, filter_low, product):
    def step(point, carry):
        product[point] = dots(
            data_high[point], data_low[point], filter_high[point], filter_low[point], ((1,), (0,))
        )
        return carry

    lax.fori_loop(0, 16, step, 0)


def place_lanes(value):
    left, right = value[:, :128], value[:, 128:]
    group = lax.broadcasted_iota(jnp.int32, left.shape, 1) // 32
    left_32, right_32 = pltpu.roll(left, 96, 1), pltpu.roll(right, 32, 1)
    left_64, right_64 = pltpu.roll(left, 64, 1), pltpu.roll(right, 64, 1)
    even = jnp.where(group == 0, left, jnp.where(group == 1, left_32, jnp.where(group == 2, right_64, right_32)))
    odd = jnp.where(group == 0, left_32, jnp.where(group == 1, left_64, jnp.where(group == 2, right_32, right)))
    return jnp.concatenate([even, odd], axis=1)


def transform_filter(weight, high, low):
    def step(index, carry):
        def piece(tap):
            start = tap * 96 + index * 2
            return jnp.concatenate(
                [weight[half, pl.ds(start, 2)].reshape(16, 128) for half in range(2)], axis=1
            )

        points = both(filter_points, [[piece(3 * a + b) for b in range(3)] for a in range(3)])
        for u in range(4):
            for v in range(4):
                top, rest = split(points[u][v])
                high[4 * u + v, rows(index, 16)] = top
                low[4 * u + v, rows(index, 16)] = rest
        return carry

    lax.fori_loop(0, 48, step, 0)


def backward_points(data_high, data_low, filter_high, filter_low, product, first, last):
    def step(point, carry):
        u, v = point // 4, point % 4
        u = jnp.where(u == 0, 3, jnp.where(u == 3, 0, u))
        v = jnp.where(v == 0, 3, jnp.where(v == 3, 0, v))
        other = 4 * u + v
        total = None
        for place in range(3):
            lanes = slice(256 * place, 256 * place + 256)
            taps = slice(256 * (2 - place), 256 * (2 - place) + 256)
            term = dots(
                data_high[point, :, lanes],
                data_low[point, :, lanes],
                filter_high[other, taps],
                filter_low[other, taps],
                ((1,), (1,)),
            )
            total = term if total is None else total + term
        product[point] = total
        return carry

    lax.fori_loop(first, last, step, 0)


def twice(fill):
    return jnp.concatenate([fill, fill], axis=1)


def upstream_of(product, cotangent, filled, grid_up, up_high, up_low):
    def step(tile, carry):
        x, y = tile // 4, tile % 4
        grid = [[product[4 * u + v, rows(tile, 16)] for v in range(4)] for u in range(4)]
        sums = both(sums_of_points, grid)
        pair = []
        for i in range(2):
            line = []
            for j in range(2):
                value = sums[i][j]
                sigma = 1.0 / (1.0 + jnp.exp(-value))
                fill = twice(filled[2 * x + i, 2 * y + j])
                result = cotangent[2 * x + i, 2 * y + j] * sigma * (1.0 + value * (1.0 - sigma)) * fill
                grid_up[2 * x + i + 1, 2 * y + j + 1] = result
                line.append(place_lanes(result))
            pair.append(line)
        points = both(points_of_pair, pair)
        for u in range(4):
            for v in range(4):
                top, rest = split(points[u][v])
                up_high[4 * u + v, rows(tile, 16)] = top
                up_low[4 * u + v, rows(tile, 16)] = rest
        return carry

    lax.fori_loop(0, 16, step, 0)


def weight_points(data_high, data_low, up_high, up_low, product, place, first, count):
    lanes = slice(256 * place, 256 * place + 256)

    def step(index, carry):
        for each in range(4):
            point = first + 4 * index + each
            product[4 * index + each] = dots(
                data_high[point, :, lanes], data_low[point, :, lanes], up_high[point], up_low[point], ((0,), (0,))
            )
        return carry

    lax.fori_loop(0, count // 4, step, 0)


def store_taps(term, a, place, index, taps, add):
    for b in range(3):
        start = ((3 * a + b) * 3 + place) * 32 + 2 * index
        for half in range(2):
            value = taps[b][:, 128 * half : 128 * half + 128].reshape(2, 8, 128)
            if add:
                value = value + term[half, pl.ds(start, 2)]
            term[half, pl.ds(start, 2)] = value


def middle_taps(product, term, place):
    def step(index, carry):
        one = [product[v, rows(index, 16)] for v in range(4)]
        two = [product[4 + v, rows(index, 16)] for v in range(4)]
        outer = taps_of_points(*[(p + q) * 0.5 for p, q in zip(one, two)])
        inner = taps_of_points(*[(p - q) * 0.5 for p, q in zip(one, two)])
        store_taps(term, 0, place, index, outer, False)
        store_taps(term, 1, place, index, inner, False)
        store_taps(term, 2, place, index, outer, False)
        return carry

    lax.fori_loop(0, 16, step, 0)


def outer_taps(product, term, place, a):
    def step(index, carry):
        taps = taps_of_points(*[product[v, rows(index, 16)] for v in range(4)])
        store_taps(term, a, place, index, taps, True)
        return carry

    lax.fori_loop(0, 16, step, 0)


def result_of(product, filled, result):
    def step(tile, carry):
        x, y = tile // 4, tile % 4
        grid = [[product[4 * u + v, rows(tile, 16)] for v in range(4)] for u in range(4)]
        sums = both(sums_of_points, grid)
        for i in range(2):
            for j in range(2):
                result[2 * x + i, 2 * y + j] = sums[i][j] * twice(filled[2 * x + i, 2 * y + j])
        return carry

    lax.fori_loop(0, 16, step, 0)


def fill_at(level, y):
    same = lax.broadcasted_iota(jnp.int32, (16, 16), 0) == lax.broadcasted_iota(jnp.int32, (16, 16), 1)
    line = jnp.where(same, jnp.broadcast_to(level[y : y + 1], (16, 16)), 0.0)
    return jnp.broadcast_to(jnp.sum(line, axis=1, keepdims=True), (16, 128))


def fill_of(occupancy, filled):
    def step(x, carry):
        level = occupancy[x].astype(F32)
        for y in range(8):
            filled[x, y] = fill_at(level, y)
        return carry

    lax.fori_loop(0, 8, step, 0)


def mask_data(padded, filled):
    def step(index, carry):
        x, y = index // 8, index % 8
        padded[x + 1, y + 1] = padded[x + 1, y + 1] * twice(filled[x, y])
        return carry

    lax.fori_loop(0, 64, step, 0)


MESH = pl.DeviceIdType.MESH
AXES = (("x", "y", "z"), ("z", "x", "y"), ("y", "z", "x"))
AROUND = [(i, j) for i in (-1, 0, 1) for j in (-1, 0, 1) if (i, j) != (0, 0)]


def wait_bytes(ref, semaphore):
    pltpu.make_async_copy(ref, ref, semaphore).wait()


FROM = {-1: lambda start: start, 0: lambda start: pl.ds(start, 8), 1: lambda start: start + 7}
TO = {-1: 9, 0: pl.ds(1, 8), 1: 0}


def border_copies(source, grid, send, side_recv, rest_recv, gx, gy, start=0):
    copies = []
    for i, j in AROUND:
        copies.append(
            pltpu.make_async_remote_copy(
                source.at[FROM[i](start), FROM[j](start)],
                grid.at[TO[i], TO[j]],
                send,
                side_recv if i == 0 else rest_recv,
                device_id=((gx + i + 16) % 16, (gy + j + 8) % 8),
                device_id_type=MESH,
            )
        )
    return copies


def level_copies(occupancy, levels, send, recv, gx, gy):
    copies = []
    for index, (i, j) in enumerate(AROUND):
        rows_x = pl.ds(0, 8) if i == 0 else pl.ds(FROM[i](0), 1)
        copies.append(
            pltpu.make_async_remote_copy(
                occupancy.at[rows_x],
                levels.at[index] if i == 0 else levels.at[index, pl.ds(0, 1)],
                send.at[0 if i == 0 else 1],
                recv.at[0 if i == 0 else 1],
                device_id=((gx + i + 16) % 16, (gy + j + 8) % 8),
                device_id_type=MESH,
            )
        )
    return copies


def mask_border(grid, levels, index):
    i, j = AROUND[index]

    def mask(x, y, level, row):
        grid[x, y] = grid[x, y] * twice(fill_at(level, row))

    if i == 0:
        for x in range(8):
            mask(x + 1, TO[j], levels[index, x].astype(F32), FROM[j](0))
    else:
        level = levels[index, 0].astype(F32)
        if j == 0:
            for y in range(8):
                mask(TO[i], y + 1, level, y)
        else:
            mask(TO[i], TO[j], level, FROM[j](0))


def take_sides(grid, gy, masks=None):
    for index, (i, _) in enumerate(AROUND):
        if i == 0 and masks:
            masks(index)

    def clear(y):
        for x in range(1, 9):
            grid[x, y] = jnp.zeros((16, 256), F32)

    pl.when(gy == 0)(lambda: clear(0))
    pl.when(gy == 7)(lambda: clear(9))


def take_rest(grid, gx, gy, masks=None):
    for index, (i, _) in enumerate(AROUND):
        if i != 0 and masks:
            masks(index)

    def clear(x, y):
        grid[x, y] = jnp.zeros((16, 256), F32)

    def clear_row(x):
        grid[x] = jnp.zeros((10, 16, 256), F32)

    def clear_corners(y):
        clear(0, y)
        clear(9, y)

    pl.when(gx == 0)(lambda: clear_row(0))
    pl.when(gx == 15)(lambda: clear_row(9))
    pl.when(gy == 0)(lambda: clear_corners(0))
    pl.when(gy == 7)(lambda: clear_corners(9))


def kernel(
    inputs, cotangent, weight, occupancy, result, weight_grad,
    term, fh, fl, dh, dl, eh, el, product, padded, padded_up, cot, filled, occ,
    from_core, ring_slots, cross_slots, packed, packed_in, final, across, levels,
    local, border_sem, core_send, core_recv,
    ring_send, ring_recv, cross_send, cross_recv, column_send, column_recv, level_send, level_recv,
):
    gx, gy = lax.axis_index("gx"), lax.axis_index("gy")
    z, x, y, c = gx // 4, gx % 4, gy // 2, gy % 2

    load_inputs = pltpu.make_async_copy(inputs, padded.at[pl.ds(1, 8), pl.ds(1, 8)], local.at[0])
    load_occ = pltpu.make_async_copy(occupancy, occ, local.at[1])
    load_weight = [
        pltpu.make_async_copy(weight.at[:, :, pl.ds(128 * half, 128)], term.at[half], local.at[2 + half])
        for half in range(2)
    ]
    load_cot = pltpu.make_async_copy(cotangent, cot, local.at[4])
    for copy in (load_occ, load_inputs, *load_weight, load_cot):
        copy.start()

    place = {"z": z, "x": x, "y": y}

    def at(position):
        return (4 * position["z"] + position["x"], 2 * position["y"] + c)

    def beside(axis, step):
        return at({**place, axis: (place[axis] + step + 4) % 4})

    def target_of(a, column):
        first, second, _ = AXES[a]
        unit = 16 * a + 4 * place[first] + place[second]
        return (unit // 3, 2 * column + c), unit % 3

    def source_of(slot, index):
        unit = 3 * gx + slot
        a, high, low = unit // 16, (unit % 16) // 4, unit % 4
        position = {
            axis: sum(
                jnp.where(a == part, (high, low, index)[AXES[part].index(axis)], 0) for part in range(3)
            )
            for axis in ("z", "x", "y")
        }
        return at(position)

    partners = [((gx + i + 16) % 16, (gy + j + 8) % 8) for i, j in AROUND]
    partners += [(gx, 2 * y + 1 - c)]
    partners += [beside(axis, step) for axis in ("z", "x", "y") for step in (1, -1)]
    partners += [target_of(a, column)[0] for a in range(3) for column in range(4)]
    partners += [source_of(slot, index) for slot in range(3) for index in range(4)]
    barrier = pltpu.get_barrier_semaphore()
    for partner in partners:
        pl.semaphore_signal(barrier, inc=1, device_id=partner, device_id_type=MESH)

    pl.semaphore_wait(barrier, len(partners))
    level_borders = level_copies(occupancy, levels, level_send, level_recv, gx, gy)
    borders = border_copies(inputs, padded, border_sem.at[0], border_sem.at[1], border_sem.at[2], gx, gy)
    for copy in (*level_borders, *borders):
        copy.start()
    load_occ.wait()
    fill_of(occ, filled)
    load_inputs.wait()
    mask_data(padded, filled)

    def masks(index):
        mask_border(padded, levels, index)

    for copy in load_weight:
        copy.wait()
    transform_filter(term, fh, fl)
    wait_bytes(levels.at[pl.ds(0, 2)], level_recv.at[0])
    wait_bytes(padded.at[pl.ds(0, 2), pl.ds(0, 8)], border_sem.at[1])
    take_sides(padded, gy, masks)
    data_tiles(padded, dh, dl, 4, 12)
    wait_bytes(levels.at[0, pl.ds(0, 6)], level_recv.at[1])
    wait_bytes(padded.at[pl.ds(0, 2), pl.ds(0, 10)], border_sem.at[2])
    take_rest(padded, gx, gy, masks)
    data_tiles(padded, dh, dl, 0, 4)
    data_tiles(padded, dh, dl, 12, 16)
    forward(dh, dl, fh, fl, product)
    load_cot.wait()
    upstream_of(product, cot, filled, padded_up, eh, el)
    borders = border_copies(padded_up, padded_up, border_sem.at[3], border_sem.at[4], border_sem.at[4], gx, gy, 1)
    for copy in borders:
        copy.start()

    def to_core(a, place_z, b):
        taps = pl.ds(((3 * a + b) * 3 + place_z) * 32, 32)
        return pltpu.make_async_remote_copy(
            term.at[1 - c, taps], from_core.at[taps], core_send, core_recv.at[a],
            device_id=(gx, 2 * y + 1 - c), device_id_type=MESH,
        )

    def add_core(a):
        def step(index, carry):
            tiles = pl.ds(288 * a + 16 * index, 16)
            term[c, tiles] = term[c, tiles] + from_core[tiles]
            return carry

        lax.fori_loop(0, 18, step, 0)

    def axes_of(a, path):
        first, second, _ = AXES[a]
        return (first, second) if path == 0 else (second, first)

    def tiles_of(a, path, ring, cross, start=0, size=9):
        ring, cross = (ring + 4) % 4, cross % 4
        piece = 4 * ring + cross if path == 0 else 4 * cross + ring
        return pl.ds(288 * a + 18 * piece + 9 * path + start, size)

    def ring_copy(a, path, ring, cross, slot, step):
        which = 2 * a + path
        copy = pltpu.make_async_remote_copy(
            term.at[c, tiles_of(a, path, ring, cross)], ring_slots.at[which, slot],
            ring_send, ring_recv.at[which, min(slot, 4)],
            device_id=beside(axes_of(a, path)[0], step), device_id_type=MESH,
        )
        copy.start()
        rings[which][slot] = copy

    def add_ring(a, path, ring, cross, slots):
        tiles = tiles_of(a, path, ring, cross)
        value = term[c, tiles]
        for slot in slots:
            value = value + ring_slots[2 * a + path, slot]
        term[c, tiles] = value

    rings = [{} for _ in range(6)]
    order = ((0, 2), (1, 3))

    def ring_first(a):
        for low, high in order:
            for path in range(2):
                r = place[axes_of(a, path)[0]]
                ring_copy(a, path, r + 2, low, low, 1)
                ring_copy(a, path, r + 2, high, high, -1)
        for low, high in order:
            for path in range(2):
                r = place[axes_of(a, path)[0]]
                ring_copy(a, path, r + 1, high, 4 + high, 1)
                ring_copy(a, path, r - 1, low, 8 + low, -1)

    def ring_second(a):
        for low, high in order:
            for path in range(2):
                r = place[axes_of(a, path)[0]]
                rings[2 * a + path][low].wait_recv()
                add_ring(a, path, r + 1, low, (low,))
                ring_copy(a, path, r + 1, low, 4 + low, 1)
                rings[2 * a + path][high].wait_recv()
                add_ring(a, path, r - 1, high, (high,))
                ring_copy(a, path, r - 1, high, 8 + high, -1)

    def ring_last(a):
        for path in range(2):
            wait_bytes(ring_slots.at[2 * a + path, pl.ds(4, 8)], ring_recv.at[2 * a + path, 4])
            for cross in range(4):
                add_ring(a, path, place[axes_of(a, path)[0]], cross, (4 + cross, 8 + cross))
        for step in (2, 1, 3):
            for path in range(2):
                which, (along, across) = 2 * a + path, axes_of(a, path)
                copy = pltpu.make_async_remote_copy(
                    term.at[c, tiles_of(a, path, place[along], place[across] + step)], cross_slots.at[which, step - 1],
                    cross_send, cross_recv.at[which],
                    device_id=beside(across, step), device_id_type=MESH,
                )
                copy.start()

    group = lax.broadcasted_iota(jnp.int32, (8, 128), 1) // 32
    columns = []

    def column_copy(a, column):
        target, slot = target_of(a, column)
        index = place[AXES[a][2]]
        here = jnp.logical_and(target[0] == gx, column == y)
        local_copy = pltpu.make_async_copy(
            packed.at[a, column], packed_in.at[slot, index], column_recv
        )
        copy = pltpu.make_async_remote_copy(
            packed.at[a, column], packed_in.at[slot, index], column_send.at[a, column], column_recv,
            device_id=target, device_id_type=MESH,
        )
        pl.when(here)(local_copy.start)
        pl.when(jnp.logical_not(here))(copy.start)
        columns.append((here, copy))

    def cross_last(a):
        for path in range(2):
            which = 2 * a + path
            wait_bytes(cross_slots.at[which], cross_recv.at[which])
            along, across = axes_of(a, path)
            tiles = tiles_of(a, path, place[along], place[across])
            final[pl.ds(9 * path, 9)] = (term[c, tiles] + cross_slots[which, 0]) + (
                cross_slots[which, 1] + cross_slots[which, 2]
            )
        for index in range(5):
            parts = [final[min(4 * index + q, 17)] for q in range(4)]
            for column in range(4):
                moved = [
                    part if q == column else pltpu.roll(part, (32 * (q - column)) % 128, 1)
                    for q, part in enumerate(parts)
                ]
                packed[a, column, index] = jnp.where(
                    group == 0, moved[0], jnp.where(group == 1, moved[1], jnp.where(group == 2, moved[2], moved[3]))
                )
        for column in range(4):
            column_copy(a, column)

    def weight_part(a, first, count, places=(0, 1, 2)):
        for place_z in places:
            weight_points(dh, dl, eh, el, product, place_z, first, count)
            if a == 1:
                middle_taps(product, term, place_z)
            else:
                outer_taps(product, term, place_z, a)
            for b in range(3):
                to_core(a, place_z, b).start()

    def core_sum(a):
        wait_bytes(from_core.at[pl.ds(288 * a, 288)], core_recv.at[a])
        add_core(a)

    def points(first, last):
        backward_points(dh, dl, fh, fl, product, first, last)

    weight_part(1, 4, 8)
    weight_part(0, 0, 4, (0,))
    core_sum(1)
    ring_first(1)
    weight_part(0, 0, 4, (1, 2))
    weight_part(2, 12, 4, (0,))
    core_sum(0)
    ring_first(0)
    weight_part(2, 12, 4, (1, 2))
    ring_second(1)
    wait_bytes(padded_up.at[pl.ds(0, 6), pl.ds(0, 6)], border_sem.at[4])
    take_sides(padded_up, gy)
    take_rest(padded_up, gx, gy)
    data_tiles(padded_up, dh, dl, 0, 5)
    core_sum(2)
    ring_first(2)
    data_tiles(padded_up, dh, dl, 5, 16)
    ring_second(0)
    points(0, 3)
    ring_second(2)
    points(3, 5)
    ring_last(1)
    points(5, 7)
    ring_last(0)
    points(7, 9)
    ring_last(2)
    points(9, 11)
    cross_last(1)
    points(11, 13)
    cross_last(0)
    points(13, 16)
    cross_last(2)
    result_of(product, filled, cot)
    store = pltpu.make_async_copy(cot, result, local.at[0])
    store.start()
    wait_bytes(packed_in, column_recv)
    for slot in range(3):
        for index in range(5):
            total = (packed_in[slot, 0, index] + packed_in[slot, 1, index]) + (
                packed_in[slot, 2, index] + packed_in[slot, 3, index]
            )
            for q in range(4 if index < 4 else 2):
                final[18 * slot + 4 * index + q] = total if q == 0 else pltpu.roll(total, 128 - 32 * q, 1)
    across[...] = final[...].reshape(448, 128).T[:32, :432]
    store_weight = pltpu.make_async_copy(across, weight_grad, local.at[1])
    store_weight.start()
    store.wait()
    store_weight.wait()
    wait_bytes(levels.at[pl.ds(0, 2)], level_send.at[0])
    wait_bytes(levels.at[0, pl.ds(0, 6)], level_send.at[1])
    wait_bytes(padded.at[pl.ds(0, 6), pl.ds(0, 6)], border_sem.at[0])
    wait_bytes(padded_up.at[pl.ds(0, 6), pl.ds(0, 6)], border_sem.at[3])
    wait_bytes(from_core, core_send)
    wait_bytes(ring_slots, ring_send)
    wait_bytes(cross_slots, cross_send)
    for here, copy in columns:
        pl.when(jnp.logical_not(here))(copy.wait_send)


def body(inputs, cotangent, weight, occupancy):
    anywhere = pl.BlockSpec(memory_space=pl.ANY)
    dma = pltpu.SemaphoreType.DMA
    result, weight_grad = pl.pallas_call(
        kernel,
        out_shape=(
            pltpu.VMEM((8, 8, 16, 256), F32),
            pltpu.VMEM((32, 432), F32),
        ),
        in_specs=[anywhere] * 4,
        out_specs=(anywhere, anywhere),
        scratch_shapes=[
            pltpu.VMEM((2, 864, 8, 128), F32),
            pltpu.VMEM((16, 768, 256), BF16),
            pltpu.VMEM((16, 768, 256), BF16),
            pltpu.VMEM((16, 256, 768), BF16),
            pltpu.VMEM((16, 256, 768), BF16),
            pltpu.VMEM((16, 256, 256), BF16),
            pltpu.VMEM((16, 256, 256), BF16),
            pltpu.VMEM((16, 256, 256), F32),
            pltpu.VMEM((10, 10, 16, 256), F32),
            pltpu.VMEM((10, 10, 16, 256), F32),
            pltpu.VMEM((8, 8, 16, 256), F32),
            pltpu.VMEM((8, 8, 16, 128), F32),
            pltpu.VMEM((8, 8, 16), jnp.int32),
            pltpu.VMEM((864, 8, 128), F32),
            pltpu.VMEM((6, 12, 9, 8, 128), F32),
            pltpu.VMEM((6, 3, 9, 8, 128), F32),
            pltpu.VMEM((3, 4, 5, 8, 128), F32),
            pltpu.VMEM((3, 4, 5, 8, 128), F32),
            pltpu.VMEM((56, 8, 128), F32),
            pltpu.VMEM((32, 432), F32),
            pltpu.VMEM((8, 8, 8, 16), jnp.int32),
            dma((5,)), dma((5,)), dma, dma((3,)), dma, dma((6, 5)), dma, dma((6,)),
            dma((3, 4)), dma, dma((2,)), dma((2,)),
        ],
        compiler_params=pltpu.CompilerParams(
            vmem_limit_bytes=56 << 20, collective_id=0, has_side_effects=True
        ),
        name="voxels",
    )(inputs, cotangent, weight.reshape(864, 8, 256), occupancy)
    return result, weight_grad.T


def solution(mesh):
    in_specs = (P("gx", "gy", None, None), P("gx", "gy", None, None), P(), P("gx", "gy", None))
    out_specs = (P("gx", "gy", None, None), P("gx", "gy"))
    return jax.shard_map(body, mesh=mesh, in_specs=in_specs, out_specs=out_specs, check_vma=False)
```

```python
import jax, jax.numpy as jnp
from jax import lax
from jax.experimental import pallas as pl
from jax.experimental.pallas import tpu as pltpu
from jax.sharding import PartitionSpec as P

F32 = jnp.float32
BF16 = jnp.bfloat16


def split(value):
    high = value.astype(BF16)
    return high, (value - high.astype(F32)).astype(BF16)


def rows(index, size):
    return pl.ds(pl.multiple_of(index * size, size), size)


def filter_points(a, b, c):
    outer, inner = (a + c) * 0.5, b * 0.5
    return a, outer + inner, outer - inner, c


def data_points(a, b, c, d, only=None):
    points = (lambda: a - c, lambda: b + c, lambda: c - b, lambda: b - d)
    return tuple(point() for point in points) if only is None else points[only]()


def sums_of_points(a, b, c, d):
    return a + b + c, b - c - d


def points_of_pair(a, b):
    return a, a + b, a - b, -b


def taps_of_points(a, b, c, d):
    outer = (b + c) * 0.5
    return a + outer, (b - c) * 0.5, outer + d


def both(function, grid):
    half = list(zip(*[function(*column) for column in zip(*grid)]))
    return [function(*row) for row in half]


def data_tiles(padded, high, low, first, last):
    def step(tile, carry):
        x, y = tile // 4, tile % 4
        grid = [[padded[2 * x + i, 2 * y + j] for j in range(4)] for i in range(4)]
        points = both(data_points, grid)
        zero = jnp.zeros((1, 256), F32)
        for u in range(4):
            for v in range(4):
                mid = points[u][v]
                down = jnp.concatenate([zero, mid[:15]], axis=0)
                up = jnp.concatenate([mid[1:], zero], axis=0)
                for place, piece in enumerate((down, mid, up)):
                    top, rest = split(piece)
                    high[4 * u + v, rows(tile, 16), 256 * place : 256 * place + 256] = top
                    low[4 * u + v, rows(tile, 16), 256 * place : 256 * place + 256] = rest
        return carry

    lax.fori_loop(first, last, step, 0)


def dots(left_high, left_low, right_high, right_low, numbers):
    dims = (numbers, ((), ()))
    return (
        lax.dot_general(left_high, right_high, dims, preferred_element_type=F32)
        + lax.dot_general(left_low, right_high, dims, preferred_element_type=F32)
        + lax.dot_general(left_high, right_low, dims, preferred_element_type=F32)
    )


def forward(data_high, data_low, filter_high, filter_low, product):
    def step(point, carry):
        product[point] = dots(
            data_high[point], data_low[point], filter_high[point], filter_low[point], ((1,), (0,))
        )
        return carry

    lax.fori_loop(0, 16, step, 0)


def place_lanes(value):
    left, right = value[:, :128], value[:, 128:]
    group = lax.broadcasted_iota(jnp.int32, left.shape, 1) // 32
    left_32, right_32 = pltpu.roll(left, 96, 1), pltpu.roll(right, 32, 1)
    left_64, right_64 = pltpu.roll(left, 64, 1), pltpu.roll(right, 64, 1)
    even = jnp.where(group == 0, left, jnp.where(group == 1, left_32, jnp.where(group == 2, right_64, right_32)))
    odd = jnp.where(group == 0, left_32, jnp.where(group == 1, left_64, jnp.where(group == 2, right_32, right)))
    return jnp.concatenate([even, odd], axis=1)


def transform_filter(weight, high, low):
    def step(index, carry):
        def piece(tap):
            start = tap * 96 + index * 2
            return jnp.concatenate(
                [weight[half, pl.ds(start, 2)].reshape(16, 128) for half in range(2)], axis=1
            )

        points = both(filter_points, [[piece(3 * a + b) for b in range(3)] for a in range(3)])
        for u in range(4):
            for v in range(4):
                top, rest = split(points[u][v])
                high[4 * u + v, rows(index, 16)] = top
                low[4 * u + v, rows(index, 16)] = rest
        return carry

    lax.fori_loop(0, 48, step, 0)


def backward_points(data_high, data_low, filter_high, filter_low, product, first, last):
    def step(point, carry):
        u, v = point // 4, point % 4
        u = jnp.where(u == 0, 3, jnp.where(u == 3, 0, u))
        v = jnp.where(v == 0, 3, jnp.where(v == 3, 0, v))
        other = 4 * u + v
        total = None
        for place in range(3):
            lanes = slice(256 * place, 256 * place + 256)
            taps = slice(256 * (2 - place), 256 * (2 - place) + 256)
            term = dots(
                data_high[point, :, lanes],
                data_low[point, :, lanes],
                filter_high[other, taps],
                filter_low[other, taps],
                ((1,), (1,)),
            )
            total = term if total is None else total + term
        product[point] = total
        return carry

    lax.fori_loop(first, last, step, 0)


def twice(fill):
    return jnp.concatenate([fill, fill], axis=1)


def upstream_of(product, cotangent, filled, grid_up, up_high, up_low):
    def step(tile, carry):
        x, y = tile // 4, tile % 4
        grid = [[product[4 * u + v, rows(tile, 16)] for v in range(4)] for u in range(4)]
        sums = both(sums_of_points, grid)
        pair = []
        for i in range(2):
            line = []
            for j in range(2):
                value = sums[i][j]
                sigma = 1.0 / (1.0 + jnp.exp(-value))
                fill = twice(filled[2 * x + i, 2 * y + j])
                result = cotangent[2 * x + i, 2 * y + j] * sigma * (1.0 + value * (1.0 - sigma)) * fill
                grid_up[2 * x + i + 1, 2 * y + j + 1] = result
                line.append(place_lanes(result))
            pair.append(line)
        points = both(points_of_pair, pair)
        for u in range(4):
            for v in range(4):
                top, rest = split(points[u][v])
                up_high[4 * u + v, rows(tile, 16)] = top
                up_low[4 * u + v, rows(tile, 16)] = rest
        return carry

    lax.fori_loop(0, 16, step, 0)


def weight_points(data_high, data_low, up_high, up_low, product, place, first, count):
    lanes = slice(256 * place, 256 * place + 256)

    def step(index, carry):
        for each in range(4):
            point = first + 4 * index + each
            product[4 * index + each] = dots(
                data_high[point, :, lanes], data_low[point, :, lanes], up_high[point], up_low[point], ((0,), (0,))
            )
        return carry

    lax.fori_loop(0, count // 4, step, 0)


def store_taps(term, a, place, index, taps, add):
    for b in range(3):
        start = ((3 * a + b) * 3 + place) * 32 + 2 * index
        for half in range(2):
            value = taps[b][:, 128 * half : 128 * half + 128].reshape(2, 8, 128)
            if add:
                value = value + term[half, pl.ds(start, 2)]
            term[half, pl.ds(start, 2)] = value


def middle_taps(product, term, place):
    def step(index, carry):
        one = [product[v, rows(index, 16)] for v in range(4)]
        two = [product[4 + v, rows(index, 16)] for v in range(4)]
        outer = taps_of_points(*[(p + q) * 0.5 for p, q in zip(one, two)])
        inner = taps_of_points(*[(p - q) * 0.5 for p, q in zip(one, two)])
        store_taps(term, 0, place, index, outer, False)
        store_taps(term, 1, place, index, inner, False)
        store_taps(term, 2, place, index, outer, False)
        return carry

    lax.fori_loop(0, 16, step, 0)


def outer_taps(product, term, place, a):
    def step(index, carry):
        taps = taps_of_points(*[product[v, rows(index, 16)] for v in range(4)])
        store_taps(term, a, place, index, taps, True)
        return carry

    lax.fori_loop(0, 16, step, 0)


def result_of(product, filled, result):
    def step(tile, carry):
        x, y = tile // 4, tile % 4
        grid = [[product[4 * u + v, rows(tile, 16)] for v in range(4)] for u in range(4)]
        sums = both(sums_of_points, grid)
        for i in range(2):
            for j in range(2):
                result[2 * x + i, 2 * y + j] = sums[i][j] * twice(filled[2 * x + i, 2 * y + j])
        return carry

    lax.fori_loop(0, 16, step, 0)


def fill_at(level, y):
    same = lax.broadcasted_iota(jnp.int32, (16, 16), 0) == lax.broadcasted_iota(jnp.int32, (16, 16), 1)
    line = jnp.where(same, jnp.broadcast_to(level[y : y + 1], (16, 16)), 0.0)
    return jnp.broadcast_to(jnp.sum(line, axis=1, keepdims=True), (16, 128))


def fill_of(occupancy, filled):
    def step(x, carry):
        level = occupancy[x].astype(F32)
        for y in range(8):
            filled[x, y] = fill_at(level, y)
        return carry

    lax.fori_loop(0, 8, step, 0)


def mask_data(padded, filled):
    def step(index, carry):
        x, y = index // 8, index % 8
        padded[x + 1, y + 1] = padded[x + 1, y + 1] * twice(filled[x, y])
        return carry

    lax.fori_loop(0, 64, step, 0)


def data_task(padded, high, low, u, tile):
    x, y = tile // 4, tile % 4
    points = data_points(*[
        data_points(*[padded[2 * x + i, 2 * y + j] if i in USED[u] else None for i in range(4)], only=u)
        for j in range(4)
    ])
    zero = jnp.zeros((1, 256), F32)
    for v, mid in enumerate(points):
        down = jnp.concatenate([zero, mid[:15]], axis=0)
        up = jnp.concatenate([mid[1:], zero], axis=0)
        for place, piece in enumerate((down, mid, up)):
            top, rest = split(piece)
            high[4 * u + v, 16 * tile : 16 * tile + 16, 256 * place : 256 * place + 256] = top
            low[4 * u + v, 16 * tile : 16 * tile + 16, 256 * place : 256 * place + 256] = rest


USED = ((0, 2), (1, 2), (1, 2), (1, 3))


def forward_point(data_high, data_low, filter_high, filter_low, product, point):
    product[point] = dots(
        data_high[point], data_low[point], filter_high[point], filter_low[point], ((1,), (0,))
    )


def backward_point(data_high, data_low, filter_high, filter_low, product, point):
    flip = (3, 1, 2, 0)
    other = 4 * flip[point // 4] + flip[point % 4]
    total = None
    for place in range(3):
        lanes = slice(256 * place, 256 * place + 256)
        taps = slice(256 * (2 - place), 256 * (2 - place) + 256)
        term = dots(
            data_high[point, :, lanes],
            data_low[point, :, lanes],
            filter_high[other, taps],
            filter_low[other, taps],
            ((1,), (1,)),
        )
        total = term if total is None else total + term
    product[point] = total


MESH = pl.DeviceIdType.MESH
AXES = (("x", "y", "z"), ("z", "x", "y"), ("y", "z", "x"))
AROUND = [(i, j) for i in (-1, 0, 1) for j in (-1, 0, 1) if (i, j) != (0, 0)]


def wait_bytes(ref, semaphore):
    pltpu.make_async_copy(ref, ref, semaphore).wait()


FROM = {-1: lambda start: start, 0: lambda start: pl.ds(start, 8), 1: lambda start: start + 7}
TO = {-1: 9, 0: pl.ds(1, 8), 1: 0}


def border_copies(source, grid, send, side_recv, rest_recv, gx, gy, start=0):
    copies = []
    for i, j in AROUND:
        copies.append(
            pltpu.make_async_remote_copy(
                source.at[FROM[i](start), FROM[j](start)],
                grid.at[TO[i], TO[j]],
                send,
                side_recv if i == 0 else rest_recv,
                device_id=((gx + i + 16) % 16, (gy + j + 8) % 8),
                device_id_type=MESH,
            )
        )
    return copies


def level_copies(occupancy, levels, send, recv, gx, gy):
    copies = []
    for index, (i, j) in enumerate(AROUND):
        rows_x = pl.ds(0, 8) if i == 0 else pl.ds(FROM[i](0), 1)
        copies.append(
            pltpu.make_async_remote_copy(
                occupancy.at[rows_x],
                levels.at[index] if i == 0 else levels.at[index, pl.ds(0, 1)],
                send.at[0 if i == 0 else 1],
                recv.at[0 if i == 0 else 1],
                device_id=((gx + i + 16) % 16, (gy + j + 8) % 8),
                device_id_type=MESH,
            )
        )
    return copies


def mask_border(grid, levels, index):
    i, j = AROUND[index]

    def mask(x, y, level, row):
        grid[x, y] = grid[x, y] * twice(fill_at(level, row))

    if i == 0:
        for x in range(8):
            mask(x + 1, TO[j], levels[index, x].astype(F32), FROM[j](0))
    else:
        level = levels[index, 0].astype(F32)
        if j == 0:
            for y in range(8):
                mask(TO[i], y + 1, level, y)
        else:
            mask(TO[i], TO[j], level, FROM[j](0))


def take_sides(grid, gy, masks=None):
    for index, (i, _) in enumerate(AROUND):
        if i == 0 and masks:
            masks(index)

    def clear(y):
        for x in range(1, 9):
            grid[x, y] = jnp.zeros((16, 256), F32)

    pl.when(gy == 0)(lambda: clear(0))
    pl.when(gy == 7)(lambda: clear(9))


def take_rest(grid, gx, gy, masks=None):
    for index, (i, _) in enumerate(AROUND):
        if i != 0 and masks:
            masks(index)

    def clear(x, y):
        grid[x, y] = jnp.zeros((16, 256), F32)

    def clear_row(x):
        grid[x] = jnp.zeros((10, 16, 256), F32)

    def clear_corners(y):
        clear(0, y)
        clear(9, y)

    pl.when(gx == 0)(lambda: clear_row(0))
    pl.when(gx == 15)(lambda: clear_row(9))
    pl.when(gy == 0)(lambda: clear_corners(0))
    pl.when(gy == 7)(lambda: clear_corners(9))


def kernel(
    inputs, cotangent, weight, occupancy, result, weight_grad,
    term, fh, fl, dh, dl, eh, el, product, padded, padded_up, cot, filled, occ,
    from_core, ring_slots, cross_slots, packed, packed_in, final, across, levels,
    turns, local, border_sem, core_send, core_recv,
    ring_send, ring_recv, cross_send, cross_recv, column_send, column_recv, level_send, level_recv,
):
    gx, gy = lax.axis_index("gx"), lax.axis_index("gy")
    z, x, y, c = gx // 4, gx % 4, gy // 2, gy % 2

    load_inputs = pltpu.make_async_copy(inputs, padded.at[pl.ds(1, 8), pl.ds(1, 8)], local.at[0])
    load_occ = pltpu.make_async_copy(occupancy, occ, local.at[1])
    load_weight = [
        pltpu.make_async_copy(weight.at[:, :, pl.ds(128 * half, 128)], term.at[half], local.at[2 + half])
        for half in range(2)
    ]
    load_cot = pltpu.make_async_copy(cotangent, cot, local.at[4])
    for copy in (load_occ, load_inputs, *load_weight, load_cot):
        copy.start()

    place = {"z": z, "x": x, "y": y}

    def at(position):
        return (4 * position["z"] + position["x"], 2 * position["y"] + c)

    def beside(axis, step):
        return at({**place, axis: (place[axis] + step + 4) % 4})

    def target_of(a, column):
        first, second, _ = AXES[a]
        unit = 16 * a + 4 * place[first] + place[second]
        return (unit // 3, 2 * column + c), unit % 3

    partners = [((gx + i + 16) % 16, (gy + j + 8) % 8) for i, j in AROUND]
    partners += [(gx, 2 * y + 1 - c)]
    partners += [beside(axis, step) for axis in ("z", "x", "y") for step in (1, -1)]
    barrier = pltpu.get_barrier_semaphore()
    for partner in partners:
        pl.semaphore_signal(barrier, inc=1, device_id=partner, device_id_type=MESH)

    near = [beside(axis, step) for axis in ("z", "x", "y") for step in (1, -1)]

    def tell(turn):
        for partner in near:
            pl.semaphore_signal(turns.at[turn], inc=1, device_id=partner, device_id_type=MESH)

    def hear(turn):
        pl.semaphore_wait(turns.at[turn], len(near))

    pl.semaphore_wait(barrier, len(partners))
    level_borders = level_copies(occupancy, levels, level_send, level_recv, gx, gy)
    borders = border_copies(inputs, padded, border_sem.at[0], border_sem.at[1], border_sem.at[2], gx, gy)
    for copy in (*level_borders, *borders):
        copy.start()
    tell(0)
    load_occ.wait()
    fill_of(occ, filled)
    load_inputs.wait()
    mask_data(padded, filled)

    def masks(index):
        mask_border(padded, levels, index)

    for copy in load_weight:
        copy.wait()
    transform_filter(term, fh, fl)
    wait_bytes(levels.at[pl.ds(0, 2)], level_recv.at[0])
    wait_bytes(padded.at[pl.ds(0, 2), pl.ds(0, 8)], border_sem.at[1])
    take_sides(padded, gy, masks)
    inner, outer = list(range(4, 12)), [0, 1, 2, 3, 12, 13, 14, 15]
    for u in range(2):
        for tile in inner:
            data_task(padded, dh, dl, u, tile)
    wait_bytes(levels.at[0, pl.ds(0, 6)], level_recv.at[1])
    wait_bytes(padded.at[pl.ds(0, 2), pl.ds(0, 10)], border_sem.at[2])
    take_rest(padded, gx, gy, masks)
    for tile in outer:
        data_task(padded, dh, dl, 0, tile)
    tasks = [[(1, tile) for tile in outer]] + [[(u, tile) for tile in range(16)] for u in (2, 3)] + [[]]
    for point in range(16):
        forward_point(dh, dl, fh, fl, product, point)
        todo = tasks[point // 4]
        share = len(todo) // 4
        for u, tile in todo[share * (point % 4) : share * (point % 4 + 1)]:
            data_task(padded, dh, dl, u, tile)
    load_cot.wait()
    upstream_of(product, cot, filled, padded_up, eh, el)
    borders = border_copies(padded_up, padded_up, border_sem.at[3], border_sem.at[4], border_sem.at[4], gx, gy, 1)
    for copy in borders:
        copy.start()

    def to_core(a, place_z, b):
        taps = pl.ds(((3 * a + b) * 3 + place_z) * 32, 32)
        return pltpu.make_async_remote_copy(
            term.at[1 - c, taps], from_core.at[taps], core_send, core_recv.at[a],
            device_id=(gx, 2 * y + 1 - c), device_id_type=MESH,
        )

    def add_core(a):
        def step(index, carry):
            tiles = pl.ds(288 * a + 16 * index, 16)
            term[c, tiles] = term[c, tiles] + from_core[tiles]
            return carry

        lax.fori_loop(0, 18, step, 0)

    def axes_of(a, path):
        first, second, _ = AXES[a]
        return (first, second) if path == 0 else (second, first)

    def tiles_of(a, path, ring, cross, start=0, size=9):
        ring, cross = (ring + 4) % 4, cross % 4
        piece = 4 * ring + cross if path == 0 else 4 * cross + ring
        return pl.ds(288 * a + 18 * piece + 9 * path + start, size)

    def ring_copy(a, path, ring, cross, slot, step):
        which = 2 * a + path
        copy = pltpu.make_async_remote_copy(
            term.at[c, tiles_of(a, path, ring, cross)], ring_slots.at[which, slot],
            ring_send, ring_recv.at[which, min(slot, 4)],
            device_id=beside(axes_of(a, path)[0], step), device_id_type=MESH,
        )
        copy.start()
        rings[which][slot] = copy

    def add_ring(a, path, ring, cross, slots):
        tiles = tiles_of(a, path, ring, cross)
        value = term[c, tiles]
        for slot in slots:
            value = value + ring_slots[2 * a + path, slot]
        term[c, tiles] = value

    rings = [{} for _ in range(6)]
    order = ((0, 2), (1, 3))

    def ring_first(a):
        for low, high in order:
            for path in range(2):
                r = place[axes_of(a, path)[0]]
                ring_copy(a, path, r + 2, low, low, 1)
                ring_copy(a, path, r + 2, high, high, -1)
        for low, high in order:
            for path in range(2):
                r = place[axes_of(a, path)[0]]
                ring_copy(a, path, r + 1, high, 4 + high, 1)
                ring_copy(a, path, r - 1, low, 8 + low, -1)

    def ring_second(a):
        for low, high in order:
            for path in range(2):
                r = place[axes_of(a, path)[0]]
                rings[2 * a + path][low].wait_recv()
                add_ring(a, path, r + 1, low, (low,))
                ring_copy(a, path, r + 1, low, 4 + low, 1)
                rings[2 * a + path][high].wait_recv()
                add_ring(a, path, r - 1, high, (high,))
                ring_copy(a, path, r - 1, high, 8 + high, -1)

    def ring_last(a):
        for path in range(2):
            wait_bytes(ring_slots.at[2 * a + path, pl.ds(4, 8)], ring_recv.at[2 * a + path, 4])
            for cross in range(4):
                add_ring(a, path, place[axes_of(a, path)[0]], cross, (4 + cross, 8 + cross))
        for step in (2, 1, 3):
            for path in range(2):
                which, (along, across) = 2 * a + path, axes_of(a, path)
                copy = pltpu.make_async_remote_copy(
                    term.at[c, tiles_of(a, path, place[along], place[across] + step)], cross_slots.at[which, step - 1],
                    cross_send, cross_recv.at[which],
                    device_id=beside(across, step), device_id_type=MESH,
                )
                copy.start()

    group = lax.broadcasted_iota(jnp.int32, (8, 128), 1) // 32
    columns = []

    def column_copy(a, column):
        target, slot = target_of(a, column)
        index = place[AXES[a][2]]
        here = jnp.logical_and(target[0] == gx, column == y)
        local_copy = pltpu.make_async_copy(
            packed.at[a, column], packed_in.at[slot, index], column_recv
        )
        copy = pltpu.make_async_remote_copy(
            packed.at[a, column], packed_in.at[slot, index], column_send.at[a, column], column_recv,
            device_id=target, device_id_type=MESH,
        )
        pl.when(here)(local_copy.start)
        pl.when(jnp.logical_not(here))(copy.start)
        columns.append((here, copy))

    def cross_last(a):
        for path in range(2):
            which = 2 * a + path
            wait_bytes(cross_slots.at[which], cross_recv.at[which])
            along, across = axes_of(a, path)
            tiles = tiles_of(a, path, place[along], place[across])
            final[pl.ds(9 * path, 9)] = (term[c, tiles] + cross_slots[which, 0]) + (
                cross_slots[which, 1] + cross_slots[which, 2]
            )
        for index in range(5):
            parts = [final[min(4 * index + q, 17)] for q in range(4)]
            for column in range(4):
                moved = [
                    part if q == column else pltpu.roll(part, (32 * (q - column)) % 128, 1)
                    for q, part in enumerate(parts)
                ]
                packed[a, column, index] = jnp.where(
                    group == 0, moved[0], jnp.where(group == 1, moved[1], jnp.where(group == 2, moved[2], moved[3]))
                )
        for column in range(4):
            column_copy(a, column)

    def weight_part(a, first, count, places=(0, 1, 2)):
        for place_z in places:
            weight_points(dh, dl, eh, el, product, place_z, first, count)
            if a == 1:
                middle_taps(product, term, place_z)
            else:
                outer_taps(product, term, place_z, a)
            for b in range(3):
                to_core(a, place_z, b).start()

    def core_sum(a):
        wait_bytes(from_core.at[pl.ds(288 * a, 288)], core_recv.at[a])
        add_core(a)

    def points(first, last):
        for point in range(first, last):
            backward_point(dh, dl, fh, fl, product, point)
            if point < 12:
                for tile in range(4 * (point % 4), 4 * (point % 4) + 4):
                    data_task(padded_up, dh, dl, point // 4 + 1, tile)

    weight_part(1, 4, 8)
    weight_part(0, 0, 4, (0,))
    core_sum(1)
    ring_first(1)
    hear(0)
    tell(1)
    weight_part(0, 0, 4, (1, 2))
    weight_part(2, 12, 4, (0,))
    core_sum(0)
    ring_first(0)
    hear(1)
    tell(2)
    weight_part(2, 12, 4, (1, 2))
    ring_second(1)
    wait_bytes(padded_up.at[pl.ds(0, 6), pl.ds(0, 6)], border_sem.at[4])
    take_sides(padded_up, gy)
    take_rest(padded_up, gx, gy)
    for tile in range(8):
        data_task(padded_up, dh, dl, 0, tile)
    core_sum(2)
    ring_first(2)
    hear(2)
    tell(3)
    for tile in range(8, 16):
        data_task(padded_up, dh, dl, 0, tile)
    ring_second(0)
    points(0, 3)
    ring_second(2)
    hear(3)
    tell(4)
    points(3, 5)
    ring_last(1)
    points(5, 7)
    ring_last(0)
    points(7, 9)
    ring_last(2)
    points(9, 11)
    hear(4)
    cross_last(1)
    points(11, 13)
    cross_last(0)
    points(13, 16)
    cross_last(2)
    result_of(product, filled, cot)
    store = pltpu.make_async_copy(cot, result, local.at[0])
    store.start()
    wait_bytes(packed_in, column_recv)
    for slot in range(3):
        for index in range(5):
            total = (packed_in[slot, 0, index] + packed_in[slot, 1, index]) + (
                packed_in[slot, 2, index] + packed_in[slot, 3, index]
            )
            for q in range(4 if index < 4 else 2):
                final[18 * slot + 4 * index + q] = total if q == 0 else pltpu.roll(total, 128 - 32 * q, 1)
    across[...] = final[...].reshape(448, 128).T[:32, :432]
    store_weight = pltpu.make_async_copy(across, weight_grad, local.at[1])
    store_weight.start()
    store.wait()
    store_weight.wait()
    wait_bytes(levels.at[pl.ds(0, 2)], level_send.at[0])
    wait_bytes(levels.at[0, pl.ds(0, 6)], level_send.at[1])
    wait_bytes(padded.at[pl.ds(0, 6), pl.ds(0, 6)], border_sem.at[0])
    wait_bytes(padded_up.at[pl.ds(0, 6), pl.ds(0, 6)], border_sem.at[3])
    wait_bytes(from_core, core_send)
    wait_bytes(ring_slots, ring_send)
    wait_bytes(cross_slots, cross_send)
    for here, copy in columns:
        pl.when(jnp.logical_not(here))(copy.wait_send)


def body(inputs, cotangent, weight, occupancy):
    anywhere = pl.BlockSpec(memory_space=pl.ANY)
    dma = pltpu.SemaphoreType.DMA
    result, weight_grad = pl.pallas_call(
        kernel,
        out_shape=(
            pltpu.VMEM((8, 8, 16, 256), F32),
            pltpu.VMEM((32, 432), F32),
        ),
        in_specs=[anywhere] * 4,
        out_specs=(anywhere, anywhere),
        scratch_shapes=[
            pltpu.VMEM((2, 864, 8, 128), F32),
            pltpu.VMEM((16, 768, 256), BF16),
            pltpu.VMEM((16, 768, 256), BF16),
            pltpu.VMEM((16, 256, 768), BF16),
            pltpu.VMEM((16, 256, 768), BF16),
            pltpu.VMEM((16, 256, 256), BF16),
            pltpu.VMEM((16, 256, 256), BF16),
            pltpu.VMEM((16, 256, 256), F32),
            pltpu.VMEM((10, 10, 16, 256), F32),
            pltpu.VMEM((10, 10, 16, 256), F32),
            pltpu.VMEM((8, 8, 16, 256), F32),
            pltpu.VMEM((8, 8, 16, 128), F32),
            pltpu.VMEM((8, 8, 16), jnp.int32),
            pltpu.VMEM((864, 8, 128), F32),
            pltpu.VMEM((6, 12, 9, 8, 128), F32),
            pltpu.VMEM((6, 3, 9, 8, 128), F32),
            pltpu.VMEM((3, 4, 5, 8, 128), F32),
            pltpu.VMEM((3, 4, 5, 8, 128), F32),
            pltpu.VMEM((56, 8, 128), F32),
            pltpu.VMEM((32, 432), F32),
            pltpu.VMEM((8, 8, 8, 16), jnp.int32),
            pltpu.SemaphoreType.REGULAR((5,)), dma((5,)), dma((5,)), dma, dma((3,)), dma, dma((6, 5)), dma, dma((6,)),
            dma((3, 4)), dma, dma((2,)), dma((2,)),
        ],
        compiler_params=pltpu.CompilerParams(
            vmem_limit_bytes=56 << 20, collective_id=0, has_side_effects=True
        ),
        name="voxels",
    )(inputs, cotangent, weight.reshape(864, 8, 256), occupancy)
    return result, weight_grad.T


def solution(mesh):
    in_specs = (P("gx", "gy", None, None), P("gx", "gy", None, None), P(), P("gx", "gy", None))
    out_specs = (P("gx", "gy", None, None), P("gx", "gy"))
    return jax.shard_map(body, mesh=mesh, in_specs=in_specs, out_specs=out_specs, check_vma=False)
```

```python
import jax, jax.numpy as jnp
from jax import lax
from jax.experimental import pallas as pl
from jax.experimental.pallas import tpu as pltpu
from jax.sharding import PartitionSpec as P

F32 = jnp.float32
BF16 = jnp.bfloat16


def split(value):
    high = value.astype(BF16)
    return high, (value - high.astype(F32)).astype(BF16)


def rows(index, size):
    return pl.ds(pl.multiple_of(index * size, size), size)


def filter_points(a, b, c):
    outer, inner = (a + c) * 0.5, b * 0.5
    return a, outer + inner, outer - inner, c


def data_points(a, b, c, d, only=None):
    points = (lambda: a - c, lambda: b + c, lambda: c - b, lambda: b - d)
    return tuple(point() for point in points) if only is None else points[only]()


def sums_of_points(a, b, c, d):
    return a + b + c, b - c - d


def points_of_pair(a, b):
    return a, a + b, a - b, -b


def taps_of_points(a, b, c, d):
    outer = (b + c) * 0.5
    return a + outer, (b - c) * 0.5, outer + d


def both(function, grid):
    half = list(zip(*[function(*column) for column in zip(*grid)]))
    return [function(*row) for row in half]


def data_tiles(padded, high, low, first, last):
    def step(tile, carry):
        x, y = tile // 4, tile % 4
        grid = [[padded[2 * x + i, 2 * y + j] for j in range(4)] for i in range(4)]
        points = both(data_points, grid)
        zero = jnp.zeros((1, 256), F32)
        for u in range(4):
            for v in range(4):
                mid = points[u][v]
                down = jnp.concatenate([zero, mid[:15]], axis=0)
                up = jnp.concatenate([mid[1:], zero], axis=0)
                for place, piece in enumerate((down, mid, up)):
                    top, rest = split(piece)
                    high[4 * u + v, rows(tile, 16), 256 * place : 256 * place + 256] = top
                    low[4 * u + v, rows(tile, 16), 256 * place : 256 * place + 256] = rest
        return carry

    lax.fori_loop(first, last, step, 0)


def dots(left_high, left_low, right_high, right_low, numbers):
    dims = (numbers, ((), ()))
    return (
        lax.dot_general(left_high, right_high, dims, preferred_element_type=F32)
        + lax.dot_general(left_low, right_high, dims, preferred_element_type=F32)
        + lax.dot_general(left_high, right_low, dims, preferred_element_type=F32)
    )


def forward(data_high, data_low, filter_high, filter_low, product):
    def step(point, carry):
        product[point] = dots(
            data_high[point], data_low[point], filter_high[point], filter_low[point], ((1,), (0,))
        )
        return carry

    lax.fori_loop(0, 16, step, 0)


def place_lanes(value):
    left, right = value[:, :128], value[:, 128:]
    group = lax.broadcasted_iota(jnp.int32, left.shape, 1) // 32
    left_32, right_32 = pltpu.roll(left, 96, 1), pltpu.roll(right, 32, 1)
    left_64, right_64 = pltpu.roll(left, 64, 1), pltpu.roll(right, 64, 1)
    even = jnp.where(group == 0, left, jnp.where(group == 1, left_32, jnp.where(group == 2, right_64, right_32)))
    odd = jnp.where(group == 0, left_32, jnp.where(group == 1, left_64, jnp.where(group == 2, right_32, right)))
    return jnp.concatenate([even, odd], axis=1)


def transform_filter(weight, high, low):
    def step(index, carry):
        def piece(tap):
            start = tap * 96 + index * 2
            return jnp.concatenate(
                [weight[half, pl.ds(start, 2)].reshape(16, 128) for half in range(2)], axis=1
            )

        points = both(filter_points, [[piece(3 * a + b) for b in range(3)] for a in range(3)])
        for u in range(4):
            for v in range(4):
                top, rest = split(points[u][v])
                high[4 * u + v, rows(index, 16)] = top
                low[4 * u + v, rows(index, 16)] = rest
        return carry

    lax.fori_loop(0, 48, step, 0)


def backward_points(data_high, data_low, filter_high, filter_low, product, first, last):
    def step(point, carry):
        u, v = point // 4, point % 4
        u = jnp.where(u == 0, 3, jnp.where(u == 3, 0, u))
        v = jnp.where(v == 0, 3, jnp.where(v == 3, 0, v))
        other = 4 * u + v
        total = None
        for place in range(3):
            lanes = slice(256 * place, 256 * place + 256)
            taps = slice(256 * (2 - place), 256 * (2 - place) + 256)
            term = dots(
                data_high[point, :, lanes],
                data_low[point, :, lanes],
                filter_high[other, taps],
                filter_low[other, taps],
                ((1,), (1,)),
            )
            total = term if total is None else total + term
        product[point] = total
        return carry

    lax.fori_loop(first, last, step, 0)


def twice(fill):
    return jnp.concatenate([fill, fill], axis=1)


def upstream_of(product, cotangent, filled, grid_up, up_high, up_low):
    def step(tile, carry):
        x, y = tile // 4, tile % 4
        grid = [[product[4 * u + v, rows(tile, 16)] for v in range(4)] for u in range(4)]
        sums = both(sums_of_points, grid)
        pair = []
        for i in range(2):
            line = []
            for j in range(2):
                value = sums[i][j]
                sigma = 1.0 / (1.0 + jnp.exp(-value))
                fill = twice(filled[2 * x + i, 2 * y + j])
                result = cotangent[2 * x + i, 2 * y + j] * sigma * (1.0 + value * (1.0 - sigma)) * fill
                grid_up[2 * x + i + 1, 2 * y + j + 1] = result
                line.append(place_lanes(result))
            pair.append(line)
        points = both(points_of_pair, pair)
        for u in range(4):
            for v in range(4):
                top, rest = split(points[u][v])
                up_high[4 * u + v, rows(tile, 16)] = top
                up_low[4 * u + v, rows(tile, 16)] = rest
        return carry

    lax.fori_loop(0, 16, step, 0)


def weight_point(data_high, data_low, up_high, up_low, product, place, point, slot):
    lanes = slice(256 * place, 256 * place + 256)
    product[slot] = dots(
        data_high[point, :, lanes], data_low[point, :, lanes], up_high[point], up_low[point], ((0,), (0,))
    )


def store_taps(term, a, place, index, taps, add):
    for b in range(3):
        start = ((3 * a + b) * 3 + place) * 32 + 2 * index
        for half in range(2):
            value = taps[b][:, 128 * half : 128 * half + 128].reshape(2, 8, 128)
            if add:
                value = value + term[half, start : start + 2]
            term[half, start : start + 2] = value


def taps_task(product, term, a, place, base, index):
    lines = slice(16 * index, 16 * index + 16)
    if a == 1:
        one = [product[base + v, lines] for v in range(4)]
        two = [product[base + 4 + v, lines] for v in range(4)]
        outer = taps_of_points(*[(p + q) * 0.5 for p, q in zip(one, two)])
        inner = taps_of_points(*[(p - q) * 0.5 for p, q in zip(one, two)])
        store_taps(term, 0, place, index, outer, False)
        store_taps(term, 1, place, index, inner, False)
        store_taps(term, 2, place, index, outer, False)
    else:
        taps = taps_of_points(*[product[base + v, lines] for v in range(4)])
        store_taps(term, a, place, index, taps, True)


def result_of(product, filled, result):
    def step(tile, carry):
        x, y = tile // 4, tile % 4
        grid = [[product[4 * u + v, rows(tile, 16)] for v in range(4)] for u in range(4)]
        sums = both(sums_of_points, grid)
        for i in range(2):
            for j in range(2):
                result[2 * x + i, 2 * y + j] = sums[i][j] * twice(filled[2 * x + i, 2 * y + j])
        return carry

    lax.fori_loop(0, 16, step, 0)


def fill_at(level, y):
    same = lax.broadcasted_iota(jnp.int32, (16, 16), 0) == lax.broadcasted_iota(jnp.int32, (16, 16), 1)
    line = jnp.where(same, jnp.broadcast_to(level[y : y + 1], (16, 16)), 0.0)
    return jnp.broadcast_to(jnp.sum(line, axis=1, keepdims=True), (16, 128))


def fill_of(occupancy, filled):
    def step(x, carry):
        level = occupancy[x].astype(F32)
        for y in range(8):
            filled[x, y] = fill_at(level, y)
        return carry

    lax.fori_loop(0, 8, step, 0)


def mask_data(padded, filled):
    def step(index, carry):
        x, y = index // 8, index % 8
        padded[x + 1, y + 1] = padded[x + 1, y + 1] * twice(filled[x, y])
        return carry

    lax.fori_loop(0, 64, step, 0)


def data_task(padded, high, low, u, tile):
    x, y = tile // 4, tile % 4
    points = data_points(*[
        data_points(*[padded[2 * x + i, 2 * y + j] if i in USED[u] else None for i in range(4)], only=u)
        for j in range(4)
    ])
    zero = jnp.zeros((1, 256), F32)
    for v, mid in enumerate(points):
        down = jnp.concatenate([zero, mid[:15]], axis=0)
        up = jnp.concatenate([mid[1:], zero], axis=0)
        for place, piece in enumerate((down, mid, up)):
            top, rest = split(piece)
            high[4 * u + v, 16 * tile : 16 * tile + 16, 256 * place : 256 * place + 256] = top
            low[4 * u + v, 16 * tile : 16 * tile + 16, 256 * place : 256 * place + 256] = rest


USED = ((0, 2), (1, 2), (1, 2), (1, 3))


def forward_point(data_high, data_low, filter_high, filter_low, product, point):
    product[point] = dots(
        data_high[point], data_low[point], filter_high[point], filter_low[point], ((1,), (0,))
    )


def backward_point(data_high, data_low, filter_high, filter_low, product, point):
    flip = (3, 1, 2, 0)
    other = 4 * flip[point // 4] + flip[point % 4]
    total = None
    for place in range(3):
        lanes = slice(256 * place, 256 * place + 256)
        taps = slice(256 * (2 - place), 256 * (2 - place) + 256)
        term = dots(
            data_high[point, :, lanes],
            data_low[point, :, lanes],
            filter_high[other, taps],
            filter_low[other, taps],
            ((1,), (1,)),
        )
        total = term if total is None else total + term
    product[point] = total


MESH = pl.DeviceIdType.MESH
AXES = (("x", "y", "z"), ("z", "x", "y"), ("y", "z", "x"))
AROUND = [(i, j) for i in (-1, 0, 1) for j in (-1, 0, 1) if (i, j) != (0, 0)]


def wait_bytes(ref, semaphore):
    pltpu.make_async_copy(ref, ref, semaphore).wait()


FROM = {-1: lambda start: start, 0: lambda start: pl.ds(start, 8), 1: lambda start: start + 7}
TO = {-1: 9, 0: pl.ds(1, 8), 1: 0}


def border_copies(source, grid, send, side_recv, rest_recv, gx, gy, start=0):
    copies = []
    for i, j in AROUND:
        copies.append(
            pltpu.make_async_remote_copy(
                source.at[FROM[i](start), FROM[j](start)],
                grid.at[TO[i], TO[j]],
                send,
                side_recv if i == 0 else rest_recv,
                device_id=((gx + i + 16) % 16, (gy + j + 8) % 8),
                device_id_type=MESH,
            )
        )
    return copies


def level_copies(occupancy, levels, send, recv, gx, gy):
    copies = []
    for index, (i, j) in enumerate(AROUND):
        rows_x = pl.ds(0, 8) if i == 0 else pl.ds(FROM[i](0), 1)
        copies.append(
            pltpu.make_async_remote_copy(
                occupancy.at[rows_x],
                levels.at[index] if i == 0 else levels.at[index, pl.ds(0, 1)],
                send.at[0 if i == 0 else 1],
                recv.at[0 if i == 0 else 1],
                device_id=((gx + i + 16) % 16, (gy + j + 8) % 8),
                device_id_type=MESH,
            )
        )
    return copies


def mask_border(grid, levels, index):
    i, j = AROUND[index]

    def mask(x, y, level, row):
        grid[x, y] = grid[x, y] * twice(fill_at(level, row))

    if i == 0:
        for x in range(8):
            mask(x + 1, TO[j], levels[index, x].astype(F32), FROM[j](0))
    else:
        level = levels[index, 0].astype(F32)
        if j == 0:
            for y in range(8):
                mask(TO[i], y + 1, level, y)
        else:
            mask(TO[i], TO[j], level, FROM[j](0))


def take_sides(grid, gy, masks=None):
    for index, (i, _) in enumerate(AROUND):
        if i == 0 and masks:
            masks(index)

    def clear(y):
        for x in range(1, 9):
            grid[x, y] = jnp.zeros((16, 256), F32)

    pl.when(gy == 0)(lambda: clear(0))
    pl.when(gy == 7)(lambda: clear(9))


def take_rest(grid, gx, gy, masks=None):
    for index, (i, _) in enumerate(AROUND):
        if i != 0 and masks:
            masks(index)

    def clear(x, y):
        grid[x, y] = jnp.zeros((16, 256), F32)

    def clear_row(x):
        grid[x] = jnp.zeros((10, 16, 256), F32)

    def clear_corners(y):
        clear(0, y)
        clear(9, y)

    pl.when(gx == 0)(lambda: clear_row(0))
    pl.when(gx == 15)(lambda: clear_row(9))
    pl.when(gy == 0)(lambda: clear_corners(0))
    pl.when(gy == 7)(lambda: clear_corners(9))


def kernel(
    inputs, cotangent, weight, occupancy, result, weight_grad,
    term, fh, fl, dh, dl, eh, el, product, padded, padded_up, cot, filled, occ,
    from_core, ring_slots, cross_slots, packed, packed_in, final, across, levels,
    turns, local, border_sem, core_send, core_recv,
    ring_send, ring_recv, cross_send, cross_recv, column_send, column_recv, level_send, level_recv,
):
    gx, gy = lax.axis_index("gx"), lax.axis_index("gy")
    z, x, y, c = gx // 4, gx % 4, gy // 2, gy % 2

    load_inputs = pltpu.make_async_copy(inputs, padded.at[pl.ds(1, 8), pl.ds(1, 8)], local.at[0])
    load_occ = pltpu.make_async_copy(occupancy, occ, local.at[1])
    load_weight = [
        pltpu.make_async_copy(weight.at[:, :, pl.ds(128 * half, 128)], term.at[half], local.at[2 + half])
        for half in range(2)
    ]
    load_cot = pltpu.make_async_copy(cotangent, cot, local.at[4])
    for copy in (load_occ, load_inputs, *load_weight, load_cot):
        copy.start()

    place = {"z": z, "x": x, "y": y}

    def at(position):
        return (4 * position["z"] + position["x"], 2 * position["y"] + c)

    def beside(axis, step):
        return at({**place, axis: (place[axis] + step + 4) % 4})

    def target_of(a, column):
        first, second, _ = AXES[a]
        unit = 16 * a + 4 * place[first] + place[second]
        return (unit // 3, 2 * column + c), unit % 3

    partners = [((gx + i + 16) % 16, (gy + j + 8) % 8) for i, j in AROUND]
    partners += [(gx, 2 * y + 1 - c)]
    partners += [beside(axis, step) for axis in ("z", "x", "y") for step in (1, -1)]
    barrier = pltpu.get_barrier_semaphore()
    for partner in partners:
        pl.semaphore_signal(barrier, inc=1, device_id=partner, device_id_type=MESH)

    near = [beside(axis, step) for axis in ("z", "x", "y") for step in (1, -1)]

    def tell(turn):
        for partner in near:
            pl.semaphore_signal(turns.at[turn], inc=1, device_id=partner, device_id_type=MESH)

    def hear(turn):
        pl.semaphore_wait(turns.at[turn], len(near))

    pl.semaphore_wait(barrier, len(partners))
    level_borders = level_copies(occupancy, levels, level_send, level_recv, gx, gy)
    borders = border_copies(inputs, padded, border_sem.at[0], border_sem.at[1], border_sem.at[2], gx, gy)
    for copy in (*level_borders, *borders):
        copy.start()
    tell(0)
    load_occ.wait()
    fill_of(occ, filled)
    load_inputs.wait()
    mask_data(padded, filled)

    def masks(index):
        mask_border(padded, levels, index)

    for copy in load_weight:
        copy.wait()
    transform_filter(term, fh, fl)
    wait_bytes(levels.at[pl.ds(0, 2)], level_recv.at[0])
    wait_bytes(padded.at[pl.ds(0, 2), pl.ds(0, 8)], border_sem.at[1])
    take_sides(padded, gy, masks)
    inner, outer = list(range(4, 12)), [0, 1, 2, 3, 12, 13, 14, 15]
    for u in range(2):
        for tile in inner:
            data_task(padded, dh, dl, u, tile)
    wait_bytes(levels.at[0, pl.ds(0, 6)], level_recv.at[1])
    wait_bytes(padded.at[pl.ds(0, 2), pl.ds(0, 10)], border_sem.at[2])
    take_rest(padded, gx, gy, masks)
    for tile in outer:
        data_task(padded, dh, dl, 0, tile)
    tasks = [[(1, tile) for tile in outer]] + [[(u, tile) for tile in range(16)] for u in (2, 3)] + [[]]
    for point in range(16):
        forward_point(dh, dl, fh, fl, product, point)
        todo = tasks[point // 4]
        share = len(todo) // 4
        for u, tile in todo[share * (point % 4) : share * (point % 4 + 1)]:
            data_task(padded, dh, dl, u, tile)
    load_cot.wait()
    upstream_of(product, cot, filled, padded_up, eh, el)
    borders = border_copies(padded_up, padded_up, border_sem.at[3], border_sem.at[4], border_sem.at[4], gx, gy, 1)
    for copy in borders:
        copy.start()

    def to_core(a, place_z, b):
        taps = pl.ds(((3 * a + b) * 3 + place_z) * 32, 32)
        return pltpu.make_async_remote_copy(
            term.at[1 - c, taps], from_core.at[taps], core_send, core_recv.at[a],
            device_id=(gx, 2 * y + 1 - c), device_id_type=MESH,
        )

    def add_core(a):
        def step(index, carry):
            tiles = pl.ds(288 * a + 16 * index, 16)
            term[c, tiles] = term[c, tiles] + from_core[tiles]
            return carry

        lax.fori_loop(0, 18, step, 0)

    def axes_of(a, path):
        first, second, _ = AXES[a]
        return (first, second) if path == 0 else (second, first)

    def tiles_of(a, path, ring, cross, start=0, size=9):
        ring, cross = (ring + 4) % 4, cross % 4
        piece = 4 * ring + cross if path == 0 else 4 * cross + ring
        return pl.ds(288 * a + 18 * piece + 9 * path + start, size)

    def ring_copy(a, path, ring, cross, slot, step):
        which = 2 * a + path
        copy = pltpu.make_async_remote_copy(
            term.at[c, tiles_of(a, path, ring, cross)], ring_slots.at[which, slot],
            ring_send, ring_recv.at[which, min(slot, 4)],
            device_id=beside(axes_of(a, path)[0], step), device_id_type=MESH,
        )
        copy.start()
        rings[which][slot] = copy

    def add_ring(a, path, ring, cross, slots):
        tiles = tiles_of(a, path, ring, cross)
        value = term[c, tiles]
        for slot in slots:
            value = value + ring_slots[2 * a + path, slot]
        term[c, tiles] = value

    rings = [{} for _ in range(6)]
    order = ((0, 2), (1, 3))

    def ring_first(a):
        for low, high in order:
            for path in range(2):
                r = place[axes_of(a, path)[0]]
                ring_copy(a, path, r + 2, low, low, 1)
                ring_copy(a, path, r + 2, high, high, -1)
        for low, high in order:
            for path in range(2):
                r = place[axes_of(a, path)[0]]
                ring_copy(a, path, r + 1, high, 4 + high, 1)
                ring_copy(a, path, r - 1, low, 8 + low, -1)

    def ring_second(a):
        for low, high in order:
            for path in range(2):
                r = place[axes_of(a, path)[0]]
                rings[2 * a + path][low].wait_recv()
                add_ring(a, path, r + 1, low, (low,))
                ring_copy(a, path, r + 1, low, 4 + low, 1)
                rings[2 * a + path][high].wait_recv()
                add_ring(a, path, r - 1, high, (high,))
                ring_copy(a, path, r - 1, high, 8 + high, -1)

    def ring_last(a):
        for path in range(2):
            wait_bytes(ring_slots.at[2 * a + path, pl.ds(4, 8)], ring_recv.at[2 * a + path, 4])
            for cross in range(4):
                add_ring(a, path, place[axes_of(a, path)[0]], cross, (4 + cross, 8 + cross))
        for step in (2, 1, 3):
            for path in range(2):
                which, (along, across) = 2 * a + path, axes_of(a, path)
                copy = pltpu.make_async_remote_copy(
                    term.at[c, tiles_of(a, path, place[along], place[across] + step)], cross_slots.at[which, step - 1],
                    cross_send, cross_recv.at[which],
                    device_id=beside(across, step), device_id_type=MESH,
                )
                copy.start()

    group = lax.broadcasted_iota(jnp.int32, (8, 128), 1) // 32
    columns = []

    def column_copy(a, column):
        target, slot = target_of(a, column)
        index = place[AXES[a][2]]
        here = jnp.logical_and(target[0] == gx, column == y)
        local_copy = pltpu.make_async_copy(
            packed.at[a, column], packed_in.at[slot, index], column_recv
        )
        copy = pltpu.make_async_remote_copy(
            packed.at[a, column], packed_in.at[slot, index], column_send.at[a, column], column_recv,
            device_id=target, device_id_type=MESH,
        )
        pl.when(here)(local_copy.start)
        pl.when(jnp.logical_not(here))(copy.start)
        columns.append((here, copy))

    def cross_last(a):
        for path in range(2):
            which = 2 * a + path
            wait_bytes(cross_slots.at[which], cross_recv.at[which])
            along, across = axes_of(a, path)
            tiles = tiles_of(a, path, place[along], place[across])
            final[pl.ds(9 * path, 9)] = (term[c, tiles] + cross_slots[which, 0]) + (
                cross_slots[which, 1] + cross_slots[which, 2]
            )
        for index in range(5):
            parts = [final[min(4 * index + q, 17)] for q in range(4)]
            for column in range(4):
                moved = [
                    part if q == column else pltpu.roll(part, (32 * (q - column)) % 128, 1)
                    for q, part in enumerate(parts)
                ]
                packed[a, column, index] = jnp.where(
                    group == 0, moved[0], jnp.where(group == 1, moved[1], jnp.where(group == 2, moved[2], moved[3]))
                )
        for column in range(4):
            column_copy(a, column)

    stages = [(a, place_z) for a in (1, 0, 2) for place_z in range(3)]

    def weight_stage(index):
        points = {1: range(4, 12), 0: range(4), 2: range(12, 16)}[stages[index][0]] if index < 9 else ()
        share = 16 // max(len(points), 1)
        for each in range(max(len(points), 1)):
            if points:
                slot = 8 * (index % 2) + each
                weight_point(dh, dl, eh, el, product, stages[index][1], points[each], slot)
            if index:
                a, place_z = stages[index - 1]
                for part in range(share * each, share * each + share):
                    taps_task(product, term, a, place_z, 8 * ((index - 1) % 2), part)
        if index:
            for b in range(3):
                to_core(*stages[index - 1], b).start()

    def core_sum(a):
        wait_bytes(from_core.at[pl.ds(288 * a, 288)], core_recv.at[a])
        add_core(a)

    def points(first, last):
        for point in range(first, last):
            backward_point(dh, dl, fh, fl, product, point)
            if point < 12:
                for tile in range(4 * (point % 4), 4 * (point % 4) + 4):
                    data_task(padded_up, dh, dl, point // 4 + 1, tile)

    for index in range(7):
        weight_stage(index)
    core_sum(1)
    ring_first(1)
    for index in range(7, 10):
        weight_stage(index)
    hear(0)
    tell(1)
    core_sum(0)
    ring_first(0)
    wait_bytes(padded_up.at[pl.ds(0, 6), pl.ds(0, 6)], border_sem.at[4])
    take_sides(padded_up, gy)
    take_rest(padded_up, gx, gy)
    for tile in range(16):
        data_task(padded_up, dh, dl, 0, tile)
    core_sum(2)
    ring_first(2)
    points(0, 3)
    ring_second(1)
    hear(1)
    tell(2)
    points(3, 8)
    ring_second(0)
    hear(2)
    tell(3)
    points(8, 11)
    ring_second(2)
    hear(3)
    tell(4)
    points(11, 13)
    ring_last(1)
    points(13, 16)
    ring_last(0)
    result_of(product, filled, cot)
    store = pltpu.make_async_copy(cot, result, local.at[0])
    store.start()
    ring_last(2)
    hear(4)
    cross_last(1)
    cross_last(0)
    cross_last(2)
    wait_bytes(packed_in, column_recv)
    for slot in range(3):
        for index in range(5):
            total = (packed_in[slot, 0, index] + packed_in[slot, 1, index]) + (
                packed_in[slot, 2, index] + packed_in[slot, 3, index]
            )
            for q in range(4 if index < 4 else 2):
                final[18 * slot + 4 * index + q] = total if q == 0 else pltpu.roll(total, 128 - 32 * q, 1)
    across[...] = final[...].reshape(448, 128).T[:32, :432]
    store_weight = pltpu.make_async_copy(across, weight_grad, local.at[1])
    store_weight.start()
    store.wait()
    store_weight.wait()
    wait_bytes(levels.at[pl.ds(0, 2)], level_send.at[0])
    wait_bytes(levels.at[0, pl.ds(0, 6)], level_send.at[1])
    wait_bytes(padded.at[pl.ds(0, 6), pl.ds(0, 6)], border_sem.at[0])
    wait_bytes(padded_up.at[pl.ds(0, 6), pl.ds(0, 6)], border_sem.at[3])
    wait_bytes(from_core, core_send)
    wait_bytes(ring_slots, ring_send)
    wait_bytes(cross_slots, cross_send)
    for here, copy in columns:
        pl.when(jnp.logical_not(here))(copy.wait_send)


def body(inputs, cotangent, weight, occupancy):
    anywhere = pl.BlockSpec(memory_space=pl.ANY)
    dma = pltpu.SemaphoreType.DMA
    result, weight_grad = pl.pallas_call(
        kernel,
        out_shape=(
            pltpu.VMEM((8, 8, 16, 256), F32),
            pltpu.VMEM((32, 432), F32),
        ),
        in_specs=[anywhere] * 4,
        out_specs=(anywhere, anywhere),
        scratch_shapes=[
            pltpu.VMEM((2, 864, 8, 128), F32),
            pltpu.VMEM((16, 768, 256), BF16),
            pltpu.VMEM((16, 768, 256), BF16),
            pltpu.VMEM((16, 256, 768), BF16),
            pltpu.VMEM((16, 256, 768), BF16),
            pltpu.VMEM((16, 256, 256), BF16),
            pltpu.VMEM((16, 256, 256), BF16),
            pltpu.VMEM((16, 256, 256), F32),
            pltpu.VMEM((10, 10, 16, 256), F32),
            pltpu.VMEM((10, 10, 16, 256), F32),
            pltpu.VMEM((8, 8, 16, 256), F32),
            pltpu.VMEM((8, 8, 16, 128), F32),
            pltpu.VMEM((8, 8, 16), jnp.int32),
            pltpu.VMEM((864, 8, 128), F32),
            pltpu.VMEM((6, 12, 9, 8, 128), F32),
            pltpu.VMEM((6, 3, 9, 8, 128), F32),
            pltpu.VMEM((3, 4, 5, 8, 128), F32),
            pltpu.VMEM((3, 4, 5, 8, 128), F32),
            pltpu.VMEM((56, 8, 128), F32),
            pltpu.VMEM((32, 432), F32),
            pltpu.VMEM((8, 8, 8, 16), jnp.int32),
            pltpu.SemaphoreType.REGULAR((5,)), dma((5,)), dma((5,)), dma, dma((3,)), dma, dma((6, 5)), dma, dma((6,)),
            dma((3, 4)), dma, dma((2,)), dma((2,)),
        ],
        compiler_params=pltpu.CompilerParams(
            vmem_limit_bytes=56 << 20, collective_id=0, has_side_effects=True
        ),
        name="voxels",
    )(inputs, cotangent, weight.reshape(864, 8, 256), occupancy)
    return result, weight_grad.T


def solution(mesh):
    in_specs = (P("gx", "gy", None, None), P("gx", "gy", None, None), P(), P("gx", "gy", None))
    out_specs = (P("gx", "gy", None, None), P("gx", "gy"))
    return jax.shard_map(body, mesh=mesh, in_specs=in_specs, out_specs=out_specs, check_vma=False)
```

```python
import jax, jax.numpy as jnp
from jax import lax
from jax.experimental import pallas as pl
from jax.experimental.pallas import tpu as pltpu
from jax.sharding import PartitionSpec as P

F32 = jnp.float32
BF16 = jnp.bfloat16


def split(value):
    high = value.astype(BF16)
    return high, (value - high.astype(F32)).astype(BF16)


def rows(index, size):
    return pl.ds(pl.multiple_of(index * size, size), size)


def filter_points(a, b, c):
    outer, inner = (a + c) * 0.5, b * 0.5
    return a, outer + inner, outer - inner, c


def data_points(a, b, c, d, only=None):
    points = (lambda: a - c, lambda: b + c, lambda: c - b, lambda: b - d)
    return tuple(point() for point in points) if only is None else points[only]()


def sums_of_points(a, b, c, d):
    return a + b + c, b - c - d


def points_of_pair(a, b):
    return a, a + b, a - b, -b


def taps_of_points(a, b, c, d):
    outer = (b + c) * 0.5
    return a + outer, (b - c) * 0.5, outer + d


def both(function, grid):
    half = list(zip(*[function(*column) for column in zip(*grid)]))
    return [function(*row) for row in half]


def data_tiles(padded, high, low, first, last):
    def step(tile, carry):
        x, y = tile // 4, tile % 4
        grid = [[padded[2 * x + i, 2 * y + j] for j in range(4)] for i in range(4)]
        points = both(data_points, grid)
        zero = jnp.zeros((1, 256), F32)
        for u in range(4):
            for v in range(4):
                mid = points[u][v]
                down = jnp.concatenate([zero, mid[:15]], axis=0)
                up = jnp.concatenate([mid[1:], zero], axis=0)
                for place, piece in enumerate((down, mid, up)):
                    top, rest = split(piece)
                    high[4 * u + v, rows(tile, 16), 256 * place : 256 * place + 256] = top
                    low[4 * u + v, rows(tile, 16), 256 * place : 256 * place + 256] = rest
        return carry

    lax.fori_loop(first, last, step, 0)


def dots(left_high, left_low, right_high, right_low, numbers):
    dims = (numbers, ((), ()))
    return (
        lax.dot_general(left_high, right_high, dims, preferred_element_type=F32)
        + lax.dot_general(left_low, right_high, dims, preferred_element_type=F32)
        + lax.dot_general(left_high, right_low, dims, preferred_element_type=F32)
    )


def forward(data_high, data_low, filter_high, filter_low, product):
    def step(point, carry):
        product[point] = dots(
            data_high[point], data_low[point], filter_high[point], filter_low[point], ((1,), (0,))
        )
        return carry

    lax.fori_loop(0, 16, step, 0)


def place_lanes(value):
    left, right = value[:, :128], value[:, 128:]
    group = lax.broadcasted_iota(jnp.int32, left.shape, 1) // 32
    left_32, right_32 = pltpu.roll(left, 96, 1), pltpu.roll(right, 32, 1)
    left_64, right_64 = pltpu.roll(left, 64, 1), pltpu.roll(right, 64, 1)
    even = jnp.where(group == 0, left, jnp.where(group == 1, left_32, jnp.where(group == 2, right_64, right_32)))
    odd = jnp.where(group == 0, left_32, jnp.where(group == 1, left_64, jnp.where(group == 2, right_32, right)))
    return jnp.concatenate([even, odd], axis=1)


def transform_filter(weight, high, low):
    def step(index, carry):
        def piece(tap):
            start = tap * 96 + index * 2
            return jnp.concatenate(
                [weight[half, pl.ds(start, 2)].reshape(16, 128) for half in range(2)], axis=1
            )

        points = both(filter_points, [[piece(3 * a + b) for b in range(3)] for a in range(3)])
        for u in range(4):
            for v in range(4):
                top, rest = split(points[u][v])
                high[4 * u + v, rows(index, 16)] = top
                low[4 * u + v, rows(index, 16)] = rest
        return carry

    lax.fori_loop(0, 48, step, 0)


def backward_points(data_high, data_low, filter_high, filter_low, product, first, last):
    def step(point, carry):
        u, v = point // 4, point % 4
        u = jnp.where(u == 0, 3, jnp.where(u == 3, 0, u))
        v = jnp.where(v == 0, 3, jnp.where(v == 3, 0, v))
        other = 4 * u + v
        total = None
        for place in range(3):
            lanes = slice(256 * place, 256 * place + 256)
            taps = slice(256 * (2 - place), 256 * (2 - place) + 256)
            term = dots(
                data_high[point, :, lanes],
                data_low[point, :, lanes],
                filter_high[other, taps],
                filter_low[other, taps],
                ((1,), (1,)),
            )
            total = term if total is None else total + term
        product[point] = total
        return carry

    lax.fori_loop(first, last, step, 0)


def twice(fill):
    return jnp.concatenate([fill, fill], axis=1)


def upstream_of(product, cotangent, filled, grid_up, up_high, up_low):
    def step(tile, carry):
        x, y = tile // 4, tile % 4
        grid = [[product[4 * u + v, rows(tile, 16)] for v in range(4)] for u in range(4)]
        sums = both(sums_of_points, grid)
        pair = []
        for i in range(2):
            line = []
            for j in range(2):
                value = sums[i][j]
                sigma = 1.0 / (1.0 + jnp.exp(-value))
                fill = twice(filled[2 * x + i, 2 * y + j])
                result = cotangent[2 * x + i, 2 * y + j] * sigma * (1.0 + value * (1.0 - sigma)) * fill
                grid_up[2 * x + i + 1, 2 * y + j + 1] = result
                line.append(place_lanes(result))
            pair.append(line)
        points = both(points_of_pair, pair)
        for u in range(4):
            for v in range(4):
                top, rest = split(points[u][v])
                up_high[4 * u + v, rows(tile, 16)] = top
                up_low[4 * u + v, rows(tile, 16)] = rest
        return carry

    lax.fori_loop(0, 16, step, 0)


def weight_point(data_high, data_low, up_high, up_low, product, place, point, slot):
    lanes = slice(256 * place, 256 * place + 256)
    product[slot] = dots(
        data_high[point, :, lanes], data_low[point, :, lanes], up_high[point], up_low[point], ((0,), (0,))
    )


def store_taps(term, a, place, index, taps, add):
    for b in range(3):
        start = ((3 * a + b) * 3 + place) * 32 + 2 * index
        for half in range(2):
            value = taps[b][:, 128 * half : 128 * half + 128].reshape(2, 8, 128)
            if add:
                value = value + term[half, start : start + 2]
            term[half, start : start + 2] = value


def taps_task(product, term, a, place, base, index):
    lines = slice(16 * index, 16 * index + 16)
    if a == 1:
        one = [product[base + v, lines] for v in range(4)]
        two = [product[base + 4 + v, lines] for v in range(4)]
        outer = taps_of_points(*[(p + q) * 0.5 for p, q in zip(one, two)])
        inner = taps_of_points(*[(p - q) * 0.5 for p, q in zip(one, two)])
        store_taps(term, 0, place, index, outer, False)
        store_taps(term, 1, place, index, inner, False)
        store_taps(term, 2, place, index, outer, False)
    else:
        taps = taps_of_points(*[product[base + v, lines] for v in range(4)])
        store_taps(term, a, place, index, taps, True)


def result_of(product, filled, result):
    def step(tile, carry):
        x, y = tile // 4, tile % 4
        grid = [[product[4 * u + v, rows(tile, 16)] for v in range(4)] for u in range(4)]
        sums = both(sums_of_points, grid)
        for i in range(2):
            for j in range(2):
                result[2 * x + i, 2 * y + j] = sums[i][j] * twice(filled[2 * x + i, 2 * y + j])
        return carry

    lax.fori_loop(0, 16, step, 0)


def fill_at(level, y):
    same = lax.broadcasted_iota(jnp.int32, (16, 16), 0) == lax.broadcasted_iota(jnp.int32, (16, 16), 1)
    line = jnp.where(same, jnp.broadcast_to(level[y : y + 1], (16, 16)), 0.0)
    return jnp.broadcast_to(jnp.sum(line, axis=1, keepdims=True), (16, 128))


def fill_of(occupancy, filled):
    def step(x, carry):
        level = occupancy[x].astype(F32)
        for y in range(8):
            filled[x, y] = fill_at(level, y)
        return carry

    lax.fori_loop(0, 8, step, 0)


def mask_data(padded, filled):
    def step(index, carry):
        x, y = index // 8, index % 8
        padded[x + 1, y + 1] = padded[x + 1, y + 1] * twice(filled[x, y])
        return carry

    lax.fori_loop(0, 64, step, 0)


def data_task(padded, high, low, u, tile):
    x, y = tile // 4, tile % 4
    points = data_points(*[
        data_points(*[padded[2 * x + i, 2 * y + j] if i in USED[u] else None for i in range(4)], only=u)
        for j in range(4)
    ])
    zero = jnp.zeros((1, 256), F32)
    for v, mid in enumerate(points):
        down = jnp.concatenate([zero, mid[:15]], axis=0)
        up = jnp.concatenate([mid[1:], zero], axis=0)
        for place, piece in enumerate((down, mid, up)):
            top, rest = split(piece)
            high[4 * u + v, 16 * tile : 16 * tile + 16, 256 * place : 256 * place + 256] = top
            low[4 * u + v, 16 * tile : 16 * tile + 16, 256 * place : 256 * place + 256] = rest


USED = ((0, 2), (1, 2), (1, 2), (1, 3))


def forward_point(data_high, data_low, filter_high, filter_low, product, point):
    product[point] = dots(
        data_high[point], data_low[point], filter_high[point], filter_low[point], ((1,), (0,))
    )


def backward_point(data_high, data_low, filter_high, filter_low, product, point):
    flip = (3, 1, 2, 0)
    other = 4 * flip[point // 4] + flip[point % 4]
    total = None
    for place in range(3):
        lanes = slice(256 * place, 256 * place + 256)
        taps = slice(256 * (2 - place), 256 * (2 - place) + 256)
        term = dots(
            data_high[point, :, lanes],
            data_low[point, :, lanes],
            filter_high[other, taps],
            filter_low[other, taps],
            ((1,), (1,)),
        )
        total = term if total is None else total + term
    product[point] = total


MESH = pl.DeviceIdType.MESH
AXES = (("x", "y", "z"), ("z", "x", "y"), ("y", "z", "x"))
AROUND = [(i, j) for i in (-1, 0, 1) for j in (-1, 0, 1) if (i, j) != (0, 0)]


def wait_bytes(ref, semaphore):
    pltpu.make_async_copy(ref, ref, semaphore).wait()


FROM = {-1: lambda start: start, 0: lambda start: pl.ds(start, 8), 1: lambda start: start + 7}
TO = {-1: 9, 0: pl.ds(1, 8), 1: 0}


def border_copies(source, grid, send, side_recv, rest_recv, gx, gy, start=0):
    copies = []
    for i, j in AROUND:
        copies.append(
            pltpu.make_async_remote_copy(
                source.at[FROM[i](start), FROM[j](start)],
                grid.at[TO[i], TO[j]],
                send,
                side_recv if i == 0 else rest_recv,
                device_id=((gx + i + 16) % 16, (gy + j + 8) % 8),
                device_id_type=MESH,
            )
        )
    return copies


def level_copies(occupancy, levels, send, recv, gx, gy):
    copies = []
    for index, (i, j) in enumerate(AROUND):
        rows_x = pl.ds(0, 8) if i == 0 else pl.ds(FROM[i](0), 1)
        copies.append(
            pltpu.make_async_remote_copy(
                occupancy.at[rows_x],
                levels.at[index] if i == 0 else levels.at[index, pl.ds(0, 1)],
                send.at[0 if i == 0 else 1],
                recv.at[0 if i == 0 else 1],
                device_id=((gx + i + 16) % 16, (gy + j + 8) % 8),
                device_id_type=MESH,
            )
        )
    return copies


def mask_border(grid, levels, index):
    i, j = AROUND[index]

    def mask(x, y, level, row):
        grid[x, y] = grid[x, y] * twice(fill_at(level, row))

    if i == 0:
        for x in range(8):
            mask(x + 1, TO[j], levels[index, x].astype(F32), FROM[j](0))
    else:
        level = levels[index, 0].astype(F32)
        if j == 0:
            for y in range(8):
                mask(TO[i], y + 1, level, y)
        else:
            mask(TO[i], TO[j], level, FROM[j](0))


def take_sides(grid, gy, masks=None):
    for index, (i, _) in enumerate(AROUND):
        if i == 0 and masks:
            masks(index)

    def clear(y):
        for x in range(1, 9):
            grid[x, y] = jnp.zeros((16, 256), F32)

    pl.when(gy == 0)(lambda: clear(0))
    pl.when(gy == 7)(lambda: clear(9))


def take_rest(grid, gx, gy, masks=None):
    for index, (i, _) in enumerate(AROUND):
        if i != 0 and masks:
            masks(index)

    def clear(x, y):
        grid[x, y] = jnp.zeros((16, 256), F32)

    def clear_row(x):
        grid[x] = jnp.zeros((10, 16, 256), F32)

    def clear_corners(y):
        clear(0, y)
        clear(9, y)

    pl.when(gx == 0)(lambda: clear_row(0))
    pl.when(gx == 15)(lambda: clear_row(9))
    pl.when(gy == 0)(lambda: clear_corners(0))
    pl.when(gy == 7)(lambda: clear_corners(9))


def kernel(
    inputs, cotangent, weight, occupancy, result, weight_grad,
    term, fh, fl, dh, dl, eh, el, product, padded, padded_up, cot, filled, occ,
    from_core, ring_slots, cross_slots, packed, packed_in, final, across, levels,
    turns, local, border_sem, core_send, core_recv,
    ring_send, ring_recv, cross_send, cross_recv, column_send, column_recv, level_send, level_recv,
):
    gx, gy = lax.axis_index("gx"), lax.axis_index("gy")
    z, x, y, c = gx // 4, gx % 4, gy // 2, gy % 2

    load_inputs = pltpu.make_async_copy(inputs, padded.at[pl.ds(1, 8), pl.ds(1, 8)], local.at[0])
    load_occ = pltpu.make_async_copy(occupancy, occ, local.at[1])
    load_weight = [
        pltpu.make_async_copy(weight.at[:, :, pl.ds(128 * half, 128)], term.at[half], local.at[2 + half])
        for half in range(2)
    ]
    load_cot = pltpu.make_async_copy(cotangent, cot, local.at[4])
    for copy in (load_occ, load_inputs, *load_weight, load_cot):
        copy.start()

    place = {"z": z, "x": x, "y": y}

    def at(position):
        return (4 * position["z"] + position["x"], 2 * position["y"] + c)

    def beside(axis, step):
        return at({**place, axis: (place[axis] + step + 4) % 4})

    def target_of(a, column):
        first, second, _ = AXES[a]
        unit = 16 * a + 4 * place[first] + place[second]
        return (unit // 3, 2 * column + c), unit % 3

    partners = [((gx + i + 16) % 16, (gy + j + 8) % 8) for i, j in AROUND]
    partners += [(gx, 2 * y + 1 - c)]
    partners += [beside(axis, step) for axis in ("z", "x", "y") for step in (1, -1)]
    barrier = pltpu.get_barrier_semaphore()
    for partner in partners:
        pl.semaphore_signal(barrier, inc=1, device_id=partner, device_id_type=MESH)

    near = [beside(axis, step) for axis in ("z", "x", "y") for step in (1, -1)]

    def tell(turn):
        for partner in near:
            pl.semaphore_signal(turns.at[turn], inc=1, device_id=partner, device_id_type=MESH)

    def hear(turn):
        pl.semaphore_wait(turns.at[turn], len(near))

    pl.semaphore_wait(barrier, len(partners))
    level_borders = level_copies(occupancy, levels, level_send, level_recv, gx, gy)
    borders = border_copies(inputs, padded, border_sem.at[0], border_sem.at[1], border_sem.at[2], gx, gy)
    for copy in (*level_borders, *borders):
        copy.start()
    tell(0)
    load_occ.wait()
    fill_of(occ, filled)
    load_inputs.wait()
    mask_data(padded, filled)

    def masks(index):
        mask_border(padded, levels, index)

    for copy in load_weight:
        copy.wait()
    transform_filter(term, fh, fl)
    wait_bytes(levels.at[pl.ds(0, 2)], level_recv.at[0])
    wait_bytes(padded.at[pl.ds(0, 2), pl.ds(0, 8)], border_sem.at[1])
    take_sides(padded, gy, masks)
    inner, outer = list(range(4, 12)), [0, 1, 2, 3, 12, 13, 14, 15]
    for u in range(3):
        for tile in inner:
            data_task(padded, dh, dl, u, tile)
    wait_bytes(levels.at[0, pl.ds(0, 6)], level_recv.at[1])
    wait_bytes(padded.at[pl.ds(0, 2), pl.ds(0, 10)], border_sem.at[2])
    take_rest(padded, gx, gy, masks)
    for tile in outer:
        data_task(padded, dh, dl, 0, tile)
    tasks = [[(u, tile) for tile in outer] for u in (1, 2)] + [[(3, tile) for tile in range(16)]] + [[]]
    for point in range(16):
        forward_point(dh, dl, fh, fl, product, point)
        todo = tasks[point // 4]
        share = len(todo) // 4
        for u, tile in todo[share * (point % 4) : share * (point % 4 + 1)]:
            data_task(padded, dh, dl, u, tile)
    load_cot.wait()
    upstream_of(product, cot, filled, padded_up, eh, el)
    borders = border_copies(padded_up, padded_up, border_sem.at[3], border_sem.at[4], border_sem.at[4], gx, gy, 1)
    for copy in borders:
        copy.start()

    def to_core(a, place_z, b):
        taps = pl.ds(((3 * a + b) * 3 + place_z) * 32, 32)
        return pltpu.make_async_remote_copy(
            term.at[1 - c, taps], from_core.at[taps], core_send, core_recv.at[a],
            device_id=(gx, 2 * y + 1 - c), device_id_type=MESH,
        )

    def add_core(a):
        def step(index, carry):
            tiles = pl.ds(288 * a + 16 * index, 16)
            term[c, tiles] = term[c, tiles] + from_core[tiles]
            return carry

        lax.fori_loop(0, 18, step, 0)

    def axes_of(a, path):
        first, second, _ = AXES[a]
        return (first, second) if path == 0 else (second, first)

    def tiles_of(a, path, ring, cross, start=0, size=9):
        ring, cross = (ring + 4) % 4, cross % 4
        piece = 4 * ring + cross if path == 0 else 4 * cross + ring
        return pl.ds(288 * a + 18 * piece + 9 * path + start, size)

    def ring_copy(a, path, ring, cross, slot, step):
        which = 2 * a + path
        copy = pltpu.make_async_remote_copy(
            term.at[c, tiles_of(a, path, ring, cross)], ring_slots.at[which, slot],
            ring_send, ring_recv.at[which, min(slot, 4)],
            device_id=beside(axes_of(a, path)[0], step), device_id_type=MESH,
        )
        copy.start()
        rings[which][slot] = copy

    def add_ring(a, path, ring, cross, slots):
        tiles = tiles_of(a, path, ring, cross)
        value = term[c, tiles]
        for slot in slots:
            value = value + ring_slots[2 * a + path, slot]
        term[c, tiles] = value

    rings = [{} for _ in range(6)]
    order = ((0, 2), (1, 3))

    def ring_first(a):
        for low, high in order:
            for path in range(2):
                r = place[axes_of(a, path)[0]]
                ring_copy(a, path, r + 2, low, low, 1)
                ring_copy(a, path, r + 2, high, high, -1)
        for low, high in order:
            for path in range(2):
                r = place[axes_of(a, path)[0]]
                ring_copy(a, path, r + 1, high, 4 + high, 1)
                ring_copy(a, path, r - 1, low, 8 + low, -1)

    def ring_second(a):
        for low, high in order:
            for path in range(2):
                r = place[axes_of(a, path)[0]]
                rings[2 * a + path][low].wait_recv()
                add_ring(a, path, r + 1, low, (low,))
                ring_copy(a, path, r + 1, low, 4 + low, 1)
                rings[2 * a + path][high].wait_recv()
                add_ring(a, path, r - 1, high, (high,))
                ring_copy(a, path, r - 1, high, 8 + high, -1)

    def ring_last(a):
        for path in range(2):
            wait_bytes(ring_slots.at[2 * a + path, pl.ds(4, 8)], ring_recv.at[2 * a + path, 4])
            for cross in range(4):
                add_ring(a, path, place[axes_of(a, path)[0]], cross, (4 + cross, 8 + cross))
        for step in (2, 1, 3):
            for path in range(2):
                which, (along, across) = 2 * a + path, axes_of(a, path)
                copy = pltpu.make_async_remote_copy(
                    term.at[c, tiles_of(a, path, place[along], place[across] + step)], cross_slots.at[which, step - 1],
                    cross_send, cross_recv.at[which],
                    device_id=beside(across, step), device_id_type=MESH,
                )
                copy.start()

    group = lax.broadcasted_iota(jnp.int32, (8, 128), 1) // 32
    columns = []

    def column_copy(a, column):
        target, slot = target_of(a, column)
        index = place[AXES[a][2]]
        here = jnp.logical_and(target[0] == gx, column == y)
        local_copy = pltpu.make_async_copy(
            packed.at[a, column], packed_in.at[slot, index], column_recv
        )
        copy = pltpu.make_async_remote_copy(
            packed.at[a, column], packed_in.at[slot, index], column_send.at[a, column], column_recv,
            device_id=target, device_id_type=MESH,
        )
        pl.when(here)(local_copy.start)
        pl.when(jnp.logical_not(here))(copy.start)
        columns.append((here, copy))

    def cross_last(a):
        for path in range(2):
            which = 2 * a + path
            wait_bytes(cross_slots.at[which], cross_recv.at[which])
            along, across = axes_of(a, path)
            tiles = tiles_of(a, path, place[along], place[across])
            final[pl.ds(9 * path, 9)] = (term[c, tiles] + cross_slots[which, 0]) + (
                cross_slots[which, 1] + cross_slots[which, 2]
            )
        for index in range(5):
            parts = [final[min(4 * index + q, 17)] for q in range(4)]
            for column in range(4):
                moved = [
                    part if q == column else pltpu.roll(part, (32 * (q - column)) % 128, 1)
                    for q, part in enumerate(parts)
                ]
                packed[a, column, index] = jnp.where(
                    group == 0, moved[0], jnp.where(group == 1, moved[1], jnp.where(group == 2, moved[2], moved[3]))
                )
        for column in range(4):
            column_copy(a, column)

    stages = [(a, place_z) for a in (1, 0, 2) for place_z in range(3)]

    def weight_stage(index):
        points = {1: range(4, 12), 0: range(4), 2: range(12, 16)}[stages[index][0]] if index < 9 else ()
        share = 16 // max(len(points), 1)
        for each in range(max(len(points), 1)):
            if points:
                slot = 8 * (index % 2) + each
                weight_point(dh, dl, eh, el, product, stages[index][1], points[each], slot)
            if index:
                a, place_z = stages[index - 1]
                for part in range(share * each, share * each + share):
                    taps_task(product, term, a, place_z, 8 * ((index - 1) % 2), part)
        if index:
            for b in range(3):
                to_core(*stages[index - 1], b).start()

    def core_sum(a):
        wait_bytes(from_core.at[pl.ds(288 * a, 288)], core_recv.at[a])
        add_core(a)

    def points(first, last):
        for point in range(first, last):
            backward_point(dh, dl, fh, fl, product, point)
            if point < 12:
                for tile in range(4 * (point % 4), 4 * (point % 4) + 4):
                    data_task(padded_up, dh, dl, point // 4 + 1, tile)

    for index in range(7):
        weight_stage(index)
    core_sum(1)
    ring_first(1)
    for index in range(7, 10):
        weight_stage(index)
    hear(0)
    tell(1)
    core_sum(0)
    ring_first(0)
    wait_bytes(padded_up.at[pl.ds(0, 6), pl.ds(0, 6)], border_sem.at[4])
    take_sides(padded_up, gy)
    take_rest(padded_up, gx, gy)
    for tile in range(16):
        data_task(padded_up, dh, dl, 0, tile)
    core_sum(2)
    ring_first(2)
    points(0, 3)
    ring_second(1)
    hear(1)
    tell(2)
    points(3, 8)
    ring_second(0)
    hear(2)
    tell(3)
    points(8, 11)
    ring_second(2)
    hear(3)
    tell(4)
    points(11, 13)
    ring_last(1)
    points(13, 16)
    ring_last(0)
    result_of(product, filled, cot)
    store = pltpu.make_async_copy(cot, result, local.at[0])
    store.start()
    ring_last(2)
    hear(4)
    cross_last(1)
    cross_last(0)
    cross_last(2)
    wait_bytes(packed_in, column_recv)
    for slot in range(3):
        for index in range(5):
            total = (packed_in[slot, 0, index] + packed_in[slot, 1, index]) + (
                packed_in[slot, 2, index] + packed_in[slot, 3, index]
            )
            for q in range(4 if index < 4 else 2):
                final[18 * slot + 4 * index + q] = total if q == 0 else pltpu.roll(total, 128 - 32 * q, 1)
    across[...] = final[...].reshape(448, 128).T[:32, :432]
    store_weight = pltpu.make_async_copy(across, weight_grad, local.at[1])
    store_weight.start()
    store.wait()
    store_weight.wait()
    wait_bytes(levels.at[pl.ds(0, 2)], level_send.at[0])
    wait_bytes(levels.at[0, pl.ds(0, 6)], level_send.at[1])
    wait_bytes(padded.at[pl.ds(0, 6), pl.ds(0, 6)], border_sem.at[0])
    wait_bytes(padded_up.at[pl.ds(0, 6), pl.ds(0, 6)], border_sem.at[3])
    wait_bytes(from_core, core_send)
    wait_bytes(ring_slots, ring_send)
    wait_bytes(cross_slots, cross_send)
    for here, copy in columns:
        pl.when(jnp.logical_not(here))(copy.wait_send)


def body(inputs, cotangent, weight, occupancy):
    anywhere = pl.BlockSpec(memory_space=pl.ANY)
    dma = pltpu.SemaphoreType.DMA
    result, weight_grad = pl.pallas_call(
        kernel,
        out_shape=(
            pltpu.VMEM((8, 8, 16, 256), F32),
            pltpu.VMEM((32, 432), F32),
        ),
        in_specs=[anywhere] * 4,
        out_specs=(anywhere, anywhere),
        scratch_shapes=[
            pltpu.VMEM((2, 864, 8, 128), F32),
            pltpu.VMEM((16, 768, 256), BF16),
            pltpu.VMEM((16, 768, 256), BF16),
            pltpu.VMEM((16, 256, 768), BF16),
            pltpu.VMEM((16, 256, 768), BF16),
            pltpu.VMEM((16, 256, 256), BF16),
            pltpu.VMEM((16, 256, 256), BF16),
            pltpu.VMEM((16, 256, 256), F32),
            pltpu.VMEM((10, 10, 16, 256), F32),
            pltpu.VMEM((10, 10, 16, 256), F32),
            pltpu.VMEM((8, 8, 16, 256), F32),
            pltpu.VMEM((8, 8, 16, 128), F32),
            pltpu.VMEM((8, 8, 16), jnp.int32),
            pltpu.VMEM((864, 8, 128), F32),
            pltpu.VMEM((6, 12, 9, 8, 128), F32),
            pltpu.VMEM((6, 3, 9, 8, 128), F32),
            pltpu.VMEM((3, 4, 5, 8, 128), F32),
            pltpu.VMEM((3, 4, 5, 8, 128), F32),
            pltpu.VMEM((56, 8, 128), F32),
            pltpu.VMEM((32, 432), F32),
            pltpu.VMEM((8, 8, 8, 16), jnp.int32),
            pltpu.SemaphoreType.REGULAR((5,)), dma((5,)), dma((5,)), dma, dma((3,)), dma, dma((6, 5)), dma, dma((6,)),
            dma((3, 4)), dma, dma((2,)), dma((2,)),
        ],
        compiler_params=pltpu.CompilerParams(
            vmem_limit_bytes=56 << 20, collective_id=0, has_side_effects=True
        ),
        name="voxels",
    )(inputs, cotangent, weight.reshape(864, 8, 256), occupancy)
    return result, weight_grad.T


def solution(mesh):
    in_specs = (P("gx", "gy", None, None), P("gx", "gy", None, None), P(), P("gx", "gy", None))
    out_specs = (P("gx", "gy", None, None), P("gx", "gy"))
    return jax.shard_map(body, mesh=mesh, in_specs=in_specs, out_specs=out_specs, check_vma=False)
```
